32 devices in a mesh: dp: 4 (over z), row: 2 (over x), col: 4 (over y, core).
Axes of the slice: x: 2, y: 2, z: 4, core: 2. Of those that a mesh axis runs over, the one named last changes fastest.
Arguments:
- hidden: bfloat16 [4096, 2560], P(('dp', 'col'), 'row'), may hold values from -6 to 6
- cotangent: bfloat16 [4096, 2560], P(('dp', 'col'), 'row'), may hold values from -6 to 6
- sequence_index: int32 [4096], P('dp'), may hold values from 0 to 7, as said below
- block_index: int32 [4096], P('dp'), may hold values from 0 to 31, never falling along the last dimension, each value on 1 to 256 neighbouring positions
- attention_gain: bfloat16 [2560], P('row'), may hold values from 0.5 to 1.5
- query_down: bfloat16 [2560, 768], P('row', 'col'), may hold values from -0.125 to 0.125
- query_gain: bfloat16 [768], replicated, may hold values from 0.5 to 1.5
- query_up: bfloat16 [768, 3840], P('row', 'col'), may hold values from -0.3125 to 0.3125
- latent_down: bfloat16 [2560, 288], P('row', 'col'), may hold values from -0.125 to 0.125
- latent_gain: bfloat16 [256], replicated, may hold values from 0.5 to 1.5
- latent_up: bfloat16 [256, 5120], P(None, 'col'), may hold values from -0.5 to 0.5
- attention_out: bfloat16 [2560, 2560], P('col', 'row'), may hold values from -3 to 3
- feedforward_gain: bfloat16 [2560], P('row'), may hold values from 0.5 to 1.5
- gate_weight: bfloat16 [2560, 6400], P('row', 'col'), may hold values from -0.125 to 0.125
- up_weight: bfloat16 [2560, 6400], P('row', 'col'), may hold values from -0.125 to 0.125
- down_weight: bfloat16 [6400, 2560], P('col', 'row'), may hold values from -0.625 to 0.625
Outputs:
- output: bfloat16 [4096, 2560], P(('dp', 'col'), 'row')
- input_gradient: bfloat16 [4096, 2560], P(('dp', 'col'), 'row')
- attention_gain_gradient: float32 [2560], P('row')
- query_down_gradient: float32 [2560, 768], P('row', 'col')
- query_gain_gradient: float32 [768], replicated
- query_up_gradient: float32 [768, 3840], P('row', 'col')
- latent_down_gradient: float32 [2560, 288], P('row', 'col')
- latent_gain_gradient: float32 [256], replicated
- latent_up_gradient: float32 [256, 5120], P(None, 'col')
- attention_out_gradient: float32 [2560, 2560], P('col', 'row')
- feedforward_gain_gradient: float32 [2560], P('row')
- gate_weight_gradient: float32 [2560, 6400], P('row', 'col')
- up_weight_gradient: float32 [2560, 6400], P('row', 'col')
- down_weight_gradient: float32 [6400, 2560], P('col', 'row')
The draws below stay inside these ranges and needn't reach their ends.
Inputs may be any that keep to these rules, and one draw needn't show every extreme that they name: `sequence_index`: ids never fall along the tokens. The g-th aligned block of 1024 tokens holds exactly the sequences 2 g and 2 g + 1, each of 256 tokens or more. `block_index`: ids never fall along the tokens; each block holds 1 to 256 tokens, and some block holds exactly 256.
All inputs are finite; a program needn't handle non-finite values.
Results may differ from the reference program's by a relative error of at most 0.018.
Values may be sent and summed in bfloat16 or wider, within the bound.
No kernel may reach another device: no remote copies, remote signals or barrier semaphores. Data moves between devices by JAX's collectives and lax.ppermute only.
A program may use at most 256 MiB of HBM per device.

```python
import math
import jax
import jax.numpy as jnp
import numpy as np
from jax import lax

D = 2560
QR = 768
KVR = 256
H = 40
NOPE = 64
RD = 32
VD = 64
FF = 6400
BLOCK = 256
TOK_GRP = 1024
TOKENS = 4096


def draw_sequence_index(key, part):
    groups = TOKENS // TOK_GRP
    cuts = jax.random.randint(key, (groups,), TOK_GRP // 4, 3 * TOK_GRP // 4 + 1)
    places = jnp.arange(TOK_GRP, dtype=jnp.int32)
    later = (places[None, :] >= cuts[:, None]).astype(jnp.int32)
    numbers = 2 * jnp.arange(groups, dtype=jnp.int32)[:, None] + later
    return numbers.reshape(TOKENS)


def block_levels(rng, extent, split, smallest, top_value):
    def one(axis_at, shards_of):
        steps = jax.random.uniform(jax.random.fold_in(jax.random.fold_in(rng, 6), axis_at), (shards_of,), jnp.float32, smallest / len(split), top_value / len(split))
        return jnp.repeat(jnp.exp(steps), extent[axis_at] // shards_of).reshape((-1,) + (1,) * (len(extent) - axis_at - 1))

    level = one(*split[0])
    for cut in split[1:]:
        level = level * one(*cut)
    return level


def split_up(amount, total, reach, skew):
    weights = [(1 << 20) // math.isqrt(rank ** skew) + 1 for rank in range(2, amount + 1)]
    surplus, counts = total - reach - (amount - 1), [1] * (amount - 1)
    while surplus > 0:
        movable = [i for i in range(amount - 1) if counts[i] < reach]
        whole, left = sum([weights[i] for i in movable]), surplus
        for i in movable:
            extra = min(reach - counts[i], max(1, left * weights[i] // whole), surplus)
            counts[i] = counts[i] + extra
            surplus = surplus - extra
    return np.array([reach] + counts)


def ragged(stream_key, number_of, total, limit, lean):
    if number_of == 2:
        one = jax.random.randint(stream_key, (), max(1, total - limit), min(limit, total - 1) + 1)
        return jnp.stack([one, total - one])
    lengths = jnp.asarray(split_up(number_of, total, limit, lean), jnp.int32)
    twos = (number_of - 1) // 2
    giver, receiver = lengths[1:1 + 2 * twos:2], lengths[2:2 + 2 * twos:2]
    room = jnp.minimum(giver - 1, limit - receiver)
    passed = jax.random.randint(jax.random.fold_in(stream_key, 1), (twos,), 0, 1 << 20) % (room + 1)
    lengths = lengths.at[1:1 + 2 * twos:2].set(giver - passed).at[2:2 + 2 * twos:2].set(receiver + passed)
    return lengths[jax.random.permutation(jax.random.fold_in(stream_key, 2), number_of)]


def normal_values(stream_key, shape, width, reach, cuts=(), held_as=jnp.bfloat16):
    array = width * jax.random.normal(stream_key, shape, jnp.float32)
    if cuts:
        array = array * block_levels(stream_key, shape, cuts, -0.22, 0.18)
    return jnp.clip(array, -reach, reach).astype(held_as)


def setup_inputs(seed: int = 0) -> dict:
    splits = jax.random.split(jax.random.key(seed), 17)
    return {
        "hidden": normal_values(splits[0], (TOKENS, D), 1.0, 6.0, ((0, 16), (1, 2))),
        "cotangent": normal_values(splits[1], (TOKENS, D), 1.0, 6.0, ((0, 16), (1, 2))),
        "sequence_index": draw_sequence_index(jax.random.fold_in(splits[16], 71), 0),
        "block_index": jnp.searchsorted(jnp.cumsum(ragged(splits[3], TOKENS // (BLOCK // 2), TOKENS, BLOCK, 0)), jnp.arange(TOKENS), side="right").astype(jnp.int32),
        "attention_gain": jnp.clip(1.0 + 0.1 * jax.random.normal(splits[4], (D,), jnp.float32), 0.5, 1.5).astype(jnp.bfloat16),
        "query_down": normal_values(splits[5], (D, QR), D ** -0.5, 0.125, ((0, 2), (1, 4))),
        "query_gain": jnp.clip(1.0 + 0.1 * jax.random.normal(splits[6], (QR,), jnp.float32), 0.5, 1.5).astype(jnp.bfloat16),
        "query_up": normal_values(splits[7], (QR, H * (NOPE + RD)), (QR // 2) ** -0.5, 0.3125, ((0, 2), (1, 4))),
        "latent_down": normal_values(splits[8], (D, KVR + RD), D ** -0.5, 0.125, ((0, 2), (1, 4))),
        "latent_gain": jnp.clip(1.0 + 0.1 * jax.random.normal(splits[9], (KVR,), jnp.float32), 0.5, 1.5).astype(jnp.bfloat16),
        "latent_up": normal_values(splits[10], (KVR, H * (NOPE + VD)), (KVR // 2) ** -0.5, 0.5, ((1, 4),)),
        "attention_out": normal_values(splits[11], (H * VD, D), 4 ** -0.5, 3.0, ((0, 4), (1, 2))),
        "feedforward_gain": jnp.clip(1.0 + 0.1 * jax.random.normal(splits[12], (D,), jnp.float32), 0.5, 1.5).astype(jnp.bfloat16),
        "gate_weight": normal_values(splits[13], (D, FF), D ** -0.5, 0.125, ((0, 2), (1, 4))),
        "up_weight": normal_values(splits[14], (D, FF), D ** -0.5, 0.125, ((0, 2), (1, 4))),
        "down_weight": normal_values(splits[15], (FF, D), (FF // 64) ** -0.5, 0.625, ((0, 4), (1, 2))),
    }


@jax.custom_vjp
def low(v):
    return lax.optimization_barrier(v.astype(jnp.bfloat16)).astype(jnp.float32)

@jax.custom_vjp
def low_back(v):
    return v

def low_keep(v):
    return (low(v), None)

def low_pass(kept, grad):
    return (grad,)

def back_keep(v):
    return (v, None)

def back_low(kept, grad):
    return (low(grad),)
low.defvjp(low_keep, low_pass)
low_back.defvjp(back_keep, back_low)
EPSILON = 1e-05
RESIDUAL_SCALE = 1.4 / math.sqrt(62.0)
MASKED = -1000000000.0

def matmul(operand, other):
    return jnp.dot(operand, other, precision=lax.Precision.HIGHEST, preferred_element_type=jnp.float32)

def rms_norm(values, scaling):
    return values * lax.rsqrt(lax.optimization_barrier(jnp.mean(values * values, axis=-1, keepdims=True)) + EPSILON) * scaling

def rotate(values, cosine, sine_part):
    half_width = values.shape[-1] // 2
    first_half = values[..., :half_width]
    second_half = values[..., half_width:]
    return jnp.concatenate([first_half * cosine - second_half * sine_part, second_half * cosine + first_half * sine_part], axis=-1)

def frequencies(rotary_width):
    return jnp.exp(jnp.arange(rotary_width // 2, dtype=jnp.float32) * (-2.0 * math.log(10000.0) / rotary_width))

def attend(queries, key_nope, key_rope, values, sequence, blocks):
    row_count = queries.shape[0]
    block_rows = min(512, row_count)
    score_scale = (NOPE + RD) ** (-0.5)

    def one_block(offset):
        block_queries = lax.dynamic_slice_in_dim(queries, offset, block_rows, 0)
        block_sequence = lax.dynamic_slice_in_dim(sequence, offset, block_rows, 0)
        block_ids = lax.dynamic_slice_in_dim(blocks, offset, block_rows, 0)
        raw_dots = jnp.einsum('qhd,khd->hqk', block_queries[..., :NOPE], key_nope, precision=lax.Precision.HIGHEST)
        raw_dots = raw_dots + jnp.einsum('qhd,kd->hqk', block_queries[..., NOPE:], key_rope, precision=lax.Precision.HIGHEST)
        allowed = (block_sequence[:, None] == sequence[None, :]) & (blocks[None, :] <= block_ids[:, None])
        scores = jnp.where(allowed[None], low_back(raw_dots) * score_scale, MASKED)
        probabilities = jnp.exp(scores - jax.nn.logsumexp(scores, axis=2, keepdims=True))
        return jnp.einsum('hqk,khd->qhd', low(probabilities), values, precision=lax.Precision.HIGHEST)
    starts = jnp.arange(row_count // block_rows, dtype=jnp.int32) * block_rows
    return lax.map(jax.checkpoint(one_block), starts).reshape(row_count, H * VD)

def whole_layer(stream, params, sequence, blocks):
    attention_gain, query_down, query_gain, query_up, latent_down, latent_gain, latent_up, attention_out, feedforward_gain, gate_weight, up_weight, down_weight = params
    row_count = stream.shape[0]
    places = jnp.arange(row_count, dtype=jnp.int32)
    earlier = lax.optimization_barrier(jnp.sum((sequence[None, :] < sequence[:, None]).astype(jnp.int32), axis=1))
    angles = (places - earlier).astype(jnp.float32)[:, None] * frequencies(RD)[None, :]
    cosine = jnp.cos(angles)
    sine_part = jnp.sin(angles)
    normed = low(rms_norm(stream, attention_gain))
    query_latent = low_back(matmul(normed, query_down))
    kv_latent = low_back(matmul(normed, latent_down))
    compressed = low(rms_norm(query_latent, query_gain))
    latent = low(rms_norm(kv_latent[:, :KVR], latent_gain))
    key_rope = low(rotate(kv_latent[:, KVR:], cosine, sine_part))
    query_raw = low_back(matmul(compressed, query_up)).reshape(row_count, H, NOPE + RD)
    queries = low(jnp.concatenate([query_raw[..., :NOPE], rotate(query_raw[..., NOPE:], cosine[:, None], sine_part[:, None])], axis=-1))
    keyval = low_back(matmul(latent, latent_up)).reshape(row_count, H, NOPE + VD)
    attended = low(low_back(attend(queries, low(keyval[..., :NOPE]), key_rope, low(keyval[..., NOPE:]), sequence, blocks)))
    middle = stream + RESIDUAL_SCALE * low_back(matmul(attended, attention_out))
    normed_mid = low(rms_norm(middle, feedforward_gain))
    gate_value = low_back(matmul(normed_mid, gate_weight))
    up_value = low_back(matmul(normed_mid, up_weight))
    activation = low(jax.nn.silu(gate_value) * up_value)
    return middle + RESIDUAL_SCALE * low_back(matmul(activation, down_weight))

def reference(hidden, cotangent, sequence_index, block_index, attention_gain, query_down, query_gain, query_up, latent_down, latent_gain, latent_up, attention_out, feedforward_gain, gate_weight, up_weight, down_weight):
    params = tuple((weight.astype(jnp.float32) for weight in (attention_gain, query_down, query_gain, query_up, latent_down, latent_gain, latent_up, attention_out, feedforward_gain, gate_weight, up_weight, down_weight)))
    groups = hidden.shape[0] // TOK_GRP
    states = hidden.astype(jnp.float32).reshape(groups, TOK_GRP, D)
    cotangents = cotangent.astype(jnp.float32).reshape(groups, TOK_GRP, D)
    sequences = sequence_index.reshape(groups, TOK_GRP)
    block_groups = block_index.reshape(groups, TOK_GRP)

    def layer_step(totals, entries):
        stream, incoming, sequence, blocks = entries
        result, pullback = jax.vjp(lambda values, weights: whole_layer(values, weights, sequence, blocks), stream, params)
        stream_grad, weight_grads = pullback(incoming)
        totals = tuple((before + update for before, update in zip(totals, weight_grads)))
        return (totals, (result.astype(jnp.bfloat16), stream_grad.astype(jnp.bfloat16)))
    initial = tuple((jnp.zeros_like(weight) for weight in params))
    totals, (results, stream_grads) = lax.scan(layer_step, initial, (states, cotangents, sequences, block_groups))
    return (results.reshape(TOKENS, D), stream_grads.reshape(TOKENS, D), totals[0], totals[1], totals[2], totals[3], totals[4], totals[5], totals[6], totals[7], totals[8], totals[9], totals[10], totals[11])
```

```python
import math

import jax
import jax.numpy as jnp
from jax import lax
from jax.experimental import pallas as pl
from jax.experimental.pallas import tpu as pltpu
from jax.sharding import PartitionSpec as P

D = 2560
QR = 768
KVR = 256
NOPE = 64
RD = 32
VD = 64
SLOT = 128

EPSILON = 1e-05
RESIDUAL_SCALE = 1.4 / math.sqrt(62.0)
SCORE_SCALE = (NOPE + RD) ** (-0.5)
MASKED = -1000000000.0
F32 = jnp.float32
BF16 = jnp.bfloat16

OVER_X = ((0, 1), (1, 0))
OVER_CORE = ((0, 1), (1, 0), (2, 3), (3, 2))
OVER_Y = ((0, 2), (1, 3), (2, 0), (3, 1))
OVER_YCORE = ((0, 3), (1, 2), (2, 1), (3, 0))


def px(values):
    return lax.ppermute(values, "row", OVER_X)


def pc(values):
    return lax.ppermute(values, "col", OVER_CORE)


def py(values):
    return lax.ppermute(values, "col", OVER_Y)


def pyc(values):
    return lax.ppermute(values, "col", OVER_YCORE)


def dot(a, b, contract, out=F32):
    return lax.dot_general(a, b, ((contract[:1], contract[1:]), ((), ())), preferred_element_type=out)


def rows_at(values, start, length):
    return lax.dynamic_slice_in_dim(values, start, length, 0)


def put(target, piece, row, column):
    return lax.dynamic_update_slice(target, piece, (row, column))


def pair(first_is_own, own, other, axis):
    return jnp.where(
        first_is_own,
        jnp.concatenate([own, other], axis),
        jnp.concatenate([other, own], axis),
    )


def gather_plane(own):
    half = own.shape[0] // 2
    from_x, from_y = px(own), py(own)
    far = [py(from_x[:half]), px(from_y[half:])]
    same_core = jnp.concatenate([own, from_x, from_y] + far, 0)
    return jnp.concatenate([same_core, pc(same_core)], 0)


def scatter_plane(partial):
    rows = partial.shape[0] // 8
    half = rows // 2
    other = pc(partial[4 * rows :])
    total = (partial[: 4 * rows].astype(F32) + other.astype(F32)).astype(BF16)
    own, to_x, to_y, far = (total[i * rows : (i + 1) * rows] for i in range(4))
    for_y, for_x = px(far[:half]), py(far[half:])
    y_top = (to_y[:half].astype(F32) + for_y.astype(F32)).astype(BF16)
    x_low = (to_x[half:].astype(F32) + for_x.astype(F32)).astype(BF16)
    from_x = px(jnp.concatenate([to_x[:half], x_low], 0))
    from_y = py(jnp.concatenate([y_top, to_y[half:]], 0))
    return own.astype(F32) + from_x.astype(F32) + from_y.astype(F32)


def swap_over_x(values, dp_place, dp_size):
    if dp_size % 2:
        return px(values)
    half = values.shape[0] // 2
    odd = dp_place % 2
    mine = px(rows_at(values, odd * half, half))
    pairs = [(i, i ^ 1) for i in range(dp_size)]
    other = lax.ppermute(mine, "dp", pairs)
    return pair(odd == 0, mine, other, 0)


def total_over(values, axes, dp_size):
    if "core" in axes:
        values = values + pc(values)
    if "y" in axes:
        values = values + py(values)
    if "x" in axes:
        values = values + px(values)
    if dp_size & (dp_size - 1):
        return lax.psum(values, "dp")
    step = 1
    while step < dp_size:
        values = values + lax.ppermute(values, "dp", [(i, i ^ step) for i in range(dp_size)])
        step *= 2
    return values


def rms_norm(values, scaling):
    return values * lax.rsqrt(jnp.mean(values * values, axis=-1, keepdims=True) + EPSILON) * scaling


def rotate(values, cosine, sine_part):
    half_width = values.shape[-1] // 2
    first_half = values[..., :half_width]
    second_half = values[..., half_width:]
    return jnp.concatenate(
        [
            first_half * cosine - second_half * sine_part,
            second_half * cosine + first_half * sine_part,
        ],
        axis=-1,
    )


def turned(values, cosine, low_sine, high_sine):
    return (
        values * cosine
        + pltpu.roll(values, SLOT - RD // 2, 1) * low_sine
        + pltpu.roll(values, RD // 2, 1) * high_sine
    )


def allowed_bias(q_seq, q_block, k_seq, k_block):
    allowed = (q_seq == k_seq) & (k_block <= q_block)
    return jnp.where(allowed, 0.0, MASKED)


def attend_kernel(
    heads, comp, lat, rope, cosine, low_sine, high_sine, w_query, w_keyval, q_seq, q_block, k_seq, k_block,
    query_out, key_out, value_out, attended_out, lse_out,
):
    @pl.when(pl.program_id(0) == 0)
    def _():
        keyval = jnp.dot(lat[...], w_keyval[...], preferred_element_type=F32)
        lanes = lax.broadcasted_iota(jnp.int32, (lat.shape[0], SLOT), 1)
        for h in range(heads):
            part = keyval[:, h * SLOT : (h + 1) * SLOT]
            key_out[:, h * SLOT : (h + 1) * SLOT] = jnp.where(
                lanes < NOPE, part, rope[...].astype(F32)
            ).astype(BF16)
            value_out[:, h * VD : (h + 1) * VD] = part[:, NOPE:].astype(BF16)

    bias = allowed_bias(q_seq[...], q_block[...], k_seq[...], k_block[...])
    raw = jnp.dot(comp[...], w_query[...], preferred_element_type=F32)
    for h in range(heads):
        slot = slice(h * SLOT, (h + 1) * SLOT)
        query = turned(raw[:, slot], cosine[...], low_sine[...], high_sine[...]).astype(BF16)
        query_out[:, slot] = query
        scores = dot(query, key_out[:, slot], (1, 1)) * SCORE_SCALE + bias
        highest = jnp.max(scores, axis=1, keepdims=True)
        powers = jnp.exp(scores - highest)
        total = jnp.sum(powers, axis=1, keepdims=True)
        probs = (powers * (1.0 / total)).astype(BF16)
        result = jnp.dot(probs, value_out[:, h * VD : (h + 1) * VD], preferred_element_type=F32)
        attended_out[:, h * VD : (h + 1) * VD] = result.astype(BF16)
        lse_out[:, h : h + 1] = highest + jnp.log(total)


def attend_back_kernel(
    heads, query, key, value, lse, grad_out, cosine, low_sine, high_sine, q_seq, q_block, k_seq, k_block,
    query_grad, keyval_grad, rope_grad, key_total, value_total,
):
    step = pl.program_id(0)

    @pl.when(step == 0)
    def _():
        key_total[...] = jnp.zeros_like(key_total)
        value_total[...] = jnp.zeros_like(value_total)

    bias = allowed_bias(q_seq[...], q_block[...], k_seq[...], k_block[...])
    for h in range(heads):
        slot = slice(h * SLOT, (h + 1) * SLOT)
        narrow = slice(h * VD, (h + 1) * VD)
        scores = dot(query[:, slot], key[:, slot], (1, 1)) * SCORE_SCALE + bias
        probs = jnp.exp(scores - lse[:, h : h + 1])
        grad_probs = dot(grad_out[:, narrow], value[:, narrow], (1, 1))
        inner = jnp.sum(probs * grad_probs, axis=1, keepdims=True)
        grad_dots = (probs * (grad_probs - inner) * SCORE_SCALE).astype(BF16)
        back = jnp.dot(grad_dots, key[:, slot], preferred_element_type=F32)
        query_grad[:, slot] = turned(back, cosine[...], -low_sine[...], -high_sine[...]).astype(BF16)
        key_total[:, slot] += dot(grad_dots, query[:, slot], (0, 0))
        value_total[:, narrow] += dot(probs.astype(BF16), grad_out[:, narrow], (0, 0))

    @pl.when(step == pl.num_programs(0) - 1)
    def _():
        rope_total = jnp.zeros((key.shape[0], SLOT), F32)
        for h in range(heads):
            part = key_total[:, h * SLOT : (h + 1) * SLOT]
            rope_total = rope_total + part
            keyval_grad[:, h * SLOT : h * SLOT + NOPE] = part[:, :NOPE].astype(BF16)
            keyval_grad[:, h * SLOT + NOPE : (h + 1) * SLOT] = value_total[:, h * VD : (h + 1) * VD].astype(BF16)
        rope_grad[...] = rope_total[:, NOPE : NOPE + RD]


def row_tile(rows, width):
    return pl.BlockSpec((rows, width), lambda i: (i, 0))


def whole(shape):
    return pl.BlockSpec(shape, lambda i: (0, 0))


def attend(comp, lat, rope, turns, w_query, w_keyval, marks, heads, tile):
    rows = comp.shape[0]
    column = row_tile(tile, 1)
    line = whole((1, rows))
    return pl.pallas_call(
        lambda *refs: attend_kernel(heads, *refs),
        grid=(rows // tile,),
        in_specs=[
            row_tile(tile, QR), whole((rows, KVR)), whole((rows, SLOT)),
            row_tile(tile, SLOT), row_tile(tile, SLOT), row_tile(tile, SLOT),
            whole(w_query.shape), whole(w_keyval.shape), column, column, line, line,
        ],
        out_specs=[
            row_tile(tile, heads * SLOT), whole((rows, heads * SLOT)), whole((rows, heads * VD)),
            row_tile(tile, heads * VD), row_tile(tile, 8),
        ],
        out_shape=[
            jax.ShapeDtypeStruct((rows, heads * SLOT), BF16),
            jax.ShapeDtypeStruct((rows, heads * SLOT), BF16),
            jax.ShapeDtypeStruct((rows, heads * VD), BF16),
            jax.ShapeDtypeStruct((rows, heads * VD), BF16),
            jax.ShapeDtypeStruct((rows, 8), F32),
        ],
        compiler_params=pltpu.CompilerParams(vmem_limit_bytes=48 << 20),
        cost_estimate=pl.CostEstimate(
            flops=2 * rows * heads * (rows * 2 * SLOT + QR * SLOT), bytes_accessed=8 << 20,
            transcendentals=heads * rows * rows,
        ),
        name="attend",
    )(comp, lat, rope, *turns, w_query, w_keyval, *marks)


def attend_back(query, key, value, lse, grad_out, turns, marks, heads, tile):
    rows = query.shape[0]
    column = row_tile(tile, 1)
    line = whole((1, rows))
    return pl.pallas_call(
        lambda *refs: attend_back_kernel(heads, *refs),
        grid=(rows // tile,),
        in_specs=[
            row_tile(tile, heads * SLOT), whole((rows, heads * SLOT)), whole((rows, heads * VD)),
            row_tile(tile, 8), row_tile(tile, heads * VD),
            row_tile(tile, SLOT), row_tile(tile, SLOT), row_tile(tile, SLOT), column, column, line, line,
        ],
        out_specs=[
            row_tile(tile, heads * SLOT), whole((rows, heads * SLOT)), whole((rows, RD)),
        ],
        out_shape=[
            jax.ShapeDtypeStruct((rows, heads * SLOT), BF16),
            jax.ShapeDtypeStruct((rows, heads * SLOT), BF16),
            jax.ShapeDtypeStruct((rows, RD), F32),
        ],
        scratch_shapes=[pltpu.VMEM((rows, heads * SLOT), F32), pltpu.VMEM((rows, heads * VD), F32)],
        compiler_params=pltpu.CompilerParams(vmem_limit_bytes=48 << 20),
        cost_estimate=pl.CostEstimate(
            flops=2 * rows * heads * rows * 5 * SLOT, bytes_accessed=8 << 20, transcendentals=heads * rows * rows,
        ),
        name="attend_back",
    )(query, key, value, lse, grad_out, *turns, *marks)


def feedforward(rows, grad_rows, gate_up, down):
    units = down.shape[0]
    both = dot(gate_up, rows, (1, 1))
    return activate(both[:units], both[units:], dot(down, grad_rows, (1, 1)))


def activate(gate, up, grad_act):
    sigmoid_gate = jax.nn.sigmoid(gate)
    swish = gate * sigmoid_gate
    grad_gate = grad_act * up * sigmoid_gate * (1.0 + gate * (1.0 - sigmoid_gate))
    return (
        (swish * up).astype(BF16),
        jnp.concatenate([grad_gate.astype(BF16), (grad_act * swish).astype(BF16)], 0),
    )


def together(*values):
    return lax.optimization_barrier(values)


def per_device(
    dp_size, hidden, cotangent, sequence_index, block_index, attention_gain, query_down, query_gain, query_up,
    latent_down, latent_gain, latent_up, attention_out, feedforward_gain, gate_weight, up_weight, down_weight,
):
    dp_place, row, col = lax.axis_index("dp"), lax.axis_index("row"), lax.axis_index("col")
    first_x = row == 0
    token_rows = hidden.shape[0]
    own_rows = token_rows // 2
    group_rows = sequence_index.shape[0]
    half_width = hidden.shape[1]
    heads = query_up.shape[1] // (NOPE + RD) // 2
    units = gate_weight.shape[1] // 2
    tile = group_rows // 4
    shard_order = [(a, b) for b in (0, 2) for a in (0, 1)] + [(a, b) for b in (1, 3) for a in (0, 1)]
    places = [((col ^ b) * 2 + (row ^ a)) for a, b in shard_order]

    def half_of(values, axis, which):
        length = values.shape[axis] // 2
        return lax.dynamic_slice_in_dim(values, which * length, length, axis)

    stream = pair(first_x, half_of(hidden, 0, row), px(half_of(hidden, 0, 1 - row)), 1).astype(F32)
    latent_tile = jnp.concatenate([query_down.T, latent_down.T], 0)
    tile_width = latent_tile.shape[0]
    near_tiles = jnp.concatenate([latent_tile, py(latent_tile)], 0)
    latent_weights = jnp.concatenate([near_tiles, pc(near_tiles)], 0)

    query_columns = query_up.shape[1] // 2
    other_query = px(half_of(query_up, 1, 1 - row))
    w_query = pair(first_x, half_of(query_up, 1, row), other_query, 0)
    w_query = jnp.pad(w_query.reshape(QR, heads, NOPE + RD), ((0, 0), (0, 0), (0, SLOT - NOPE - RD)))
    w_query = w_query.reshape(QR, heads * SLOT)
    w_keyval = half_of(latent_up, 1, row)
    w_out = pair(first_x, half_of(attention_out, 0, row), px(half_of(attention_out, 0, 1 - row)), 1)

    def whole_units(tile_t):
        other = swap_over_x(rows_at(tile_t, (1 - row) * units, units), dp_place, dp_size)
        return pair(first_x, rows_at(tile_t, row * units, units), other, 1)

    gate_up = jnp.concatenate([whole_units(gate_weight.T), whole_units(up_weight.T)], 0)
    down = whole_units(down_weight)

    incoming = pair(first_x, half_of(cotangent, 0, row), px(half_of(cotangent, 0, 1 - row)), 1).astype(F32)
    grad_down_own = (RESIDUAL_SCALE * incoming).astype(BF16)
    grad_down = gather_plane(grad_down_own)
    by_factors = dp_size == 4
    every = ("dp", "row", "col")

    second = jnp.sum((sequence_index == sequence_index[0]).astype(jnp.int32))
    inverse_rate = -2.0 * math.log(10000.0) / RD

    def in_order(values):
        return jnp.concatenate([rows_at(values, place * own_rows, own_rows) for place in places], 0)

    seq_all, block_all = in_order(sequence_index), in_order(block_index)
    index_all = in_order(jnp.arange(group_rows, dtype=jnp.int32))
    position = (index_all - jnp.where(seq_all == sequence_index[0], 0, second)).astype(F32)
    lane = jnp.arange(SLOT, dtype=jnp.int32)
    turning = (lane >= NOPE) & (lane < NOPE + RD)
    rate = jnp.exp(((lane - NOPE) % (RD // 2)).astype(F32) * inverse_rate)
    angle = jnp.where(turning, rate, 0.0)[None, :] * position[:, None]
    cosine, sine = jnp.cos(angle), jnp.sin(angle)
    low_sine = jnp.where(lane < NOPE + RD // 2, -sine, 0.0)
    high_sine = jnp.where(lane >= NOPE + RD // 2, sine, 0.0)
    turns = (cosine, low_sine, high_sine)
    marks = (seq_all[:, None], block_all[:, None], seq_all[None, :], block_all[None, :])
    own_cosine = cosine[:own_rows, NOPE : NOPE + RD // 2]
    own_sine = sine[:own_rows, NOPE : NOPE + RD // 2]

    gain_in = attention_gain.astype(F32)
    inverse_in = lax.rsqrt(jnp.mean(stream * stream, axis=1) + EPSILON)
    inverse_half = pair(first_x, inverse_in, px(inverse_in[None, :])[0], 0)
    scaled_in = hidden.astype(F32) * inverse_half[:, None]
    normed_half = (scaled_in * gain_in[None, :]).astype(BF16)
    latent_part = dot(normed_half, latent_weights, (1, 1))
    latent_raw = half_of(latent_part, 0, row) + px(half_of(latent_part, 0, 1 - row))

    def in_place(values):
        blocks = [values[:, i * tile_width : (i + 1) * tile_width] for i in range(4)]
        core, high = (col % 2) == 1, (col // 2) == 1
        b0, b2, b1, b3 = blocks
        c0, c1 = jnp.where(core, b1, b0), jnp.where(core, b0, b1)
        c2, c3 = jnp.where(core, b3, b2), jnp.where(core, b2, b3)
        return (
            jnp.where(high, c2, c0), jnp.where(high, c3, c1), jnp.where(high, c0, c2), jnp.where(high, c1, c3),
        )

    blocks = in_place(latent_raw)
    query_tile = query_down.shape[1]
    query_latent = jnp.concatenate([b[:, :query_tile] for b in blocks], 1)
    kv_latent = jnp.concatenate([b[:, query_tile:] for b in blocks], 1)

    def latent_norms(query_values, key_values, query_scaling, key_scaling):
        return (
            rms_norm(query_values, query_scaling),
            rms_norm(key_values[:, :KVR], key_scaling),
            rotate(key_values[:, KVR:], own_cosine, own_sine),
        )

    own_latents, latent_back = jax.vjp(
        latent_norms, query_latent, kv_latent, query_gain.astype(F32), latent_gain.astype(F32)
    )
    latents = gather_plane(jnp.concatenate(own_latents, 1).astype(BF16))
    if by_factors:
        grad_down_late, latents = together(grad_down_own, latents)
        grads_all = lax.all_gather(grad_down_late, every, axis=0, tiled=True)
    compressed, latent = latents[:, :QR], latents[:, QR : QR + KVR]
    rope = jnp.pad(latents[:, QR + KVR :], ((0, 0), (NOPE, SLOT - NOPE - RD)))

    query, key, value, attended, lse = attend(
        compressed, latent, rope, turns, w_query, w_keyval, marks, heads, tile
    )

    middle = stream + RESIDUAL_SCALE * scatter_plane(dot(attended, w_out, (1, 0), BF16))
    gain_mid = pair(first_x, feedforward_gain, px(feedforward_gain), 0).astype(F32)
    inverse_mid = lax.rsqrt(jnp.mean(middle * middle, axis=1, keepdims=True) + EPSILON)
    scaled_mid = middle * inverse_mid
    normed_mid_own = (scaled_mid * gain_mid[None, :]).astype(BF16)
    normed_mid = gather_plane(normed_mid_own)

    if by_factors:
        rows_all = lax.all_gather(normed_mid_own, every, axis=0, tiled=True)

    activation, grad_both = feedforward(normed_mid, grad_down, gate_up, down)
    mid_part = dot(grad_both, gate_up, (0, 0), BF16)
    output_part = dot(activation, down, (0, 0), BF16)
    if by_factors:
        mid_part, grads_all = together(mid_part, grads_all)
        odd = dp_place % 2
        own_units = units // 2

        def own_half(weights):
            return rows_at(weights, odd * own_units, own_units)

        down_half = own_half(down)
        gate_up_half = jnp.concatenate([own_half(gate_up[:units]), own_half(gate_up[units:])], 0)
        grad_act_all = dot(down_half, grads_all, (1, 1))
    upstream_mid = scatter_plane(mid_part)
    if by_factors:
        upstream_mid, grad_act_all, output_part = together(upstream_mid, grad_act_all, output_part)
    weighted = upstream_mid * gain_mid[None, :]
    mean_inner = jnp.mean(weighted * scaled_mid, axis=1, keepdims=True)
    gain_mid_part = jnp.sum(upstream_mid * scaled_mid, axis=0)
    grad_middle = incoming + inverse_mid * (weighted - scaled_mid * mean_inner)
    grad_branch = gather_plane((RESIDUAL_SCALE * grad_middle).astype(BF16))

    grad_attended = dot(grad_branch, w_out, (1, 1), BF16)
    query_grad, keyval_grad, rope_grad = attend_back(
        query, key, value, lse, grad_attended, turns, marks, heads, tile
    )
    latent_grad_part = jnp.concatenate(
        [
            dot(query_grad, w_query, (1, 1), BF16),
            dot(keyval_grad, w_keyval, (1, 1), BF16),
            rope_grad.astype(BF16),
        ],
        1,
    )
    if by_factors:
        latent_grad_part, rows_all = together(latent_grad_part, rows_all)
        both_all = dot(gate_up_half, rows_all, (1, 1))
    latent_grad = scatter_plane(latent_grad_part)
    if by_factors:
        latent_grad, both_all = together(latent_grad, both_all)
    query_latent_grad, kv_latent_grad, query_gain_part, latent_gain_part = latent_back(
        (latent_grad[:, :QR], latent_grad[:, QR : QR + KVR], latent_grad[:, QR + KVR :])
    )
    kv_tile = latent_down.shape[1]
    query_low, kv_low = query_latent_grad.astype(BF16), kv_latent_grad.astype(BF16)
    inner_in = (
        jnp.sum(query_low.astype(F32) * query_latent, axis=1) + jnp.sum(kv_low.astype(F32) * kv_latent, axis=1)
    ) / D
    in_blocks = jnp.concatenate(
        [
            part
            for i in (0, 2, 1, 3)
            for part in (
                query_low[:, i * query_tile : (i + 1) * query_tile],
                kv_low[:, i * kv_tile : (i + 1) * kv_tile],
            )
        ],
        1,
    )
    g0, g1, g2, g3 = in_place(in_blocks)
    latent_low = jnp.concatenate([g0, g2, g1, g3], 1)
    latent_low = pair(first_x, latent_low, px(latent_low), 0)
    inner_half = pair(first_x, inner_in, px(inner_in[None, :])[0], 0)
    grad_normed = dot(latent_low, latent_weights, (1, 0))
    grad_middle_half = pair(
        first_x,
        half_of(grad_middle, 1, row),
        px(half_of(grad_middle, 1, 1 - row).astype(BF16)).astype(F32),
        0,
    )
    grad_in = inverse_half[:, None] * (grad_normed * gain_in[None, :] - scaled_in * inner_half[:, None])
    input_gradient = (grad_middle_half + grad_in).astype(BF16)
    gain_in_total = total_over(
        jnp.sum(grad_normed * scaled_in, axis=0).reshape(-1, SLOT), ("core", "y"), dp_size
    ).reshape(-1)

    output_own = (middle + RESIDUAL_SCALE * scatter_plane(output_part)).astype(BF16)
    output = pair(first_x, half_of(output_own, 1, row), px(half_of(output_own, 1, 1 - row)), 0)

    if by_factors:
        act_all, grad_both_all = together(*activate(both_all[:own_units], both_all[own_units:], grad_act_all))
        up_total = dot(grad_both_all[own_units:], rows_all, (1, 0), BF16)
        gate_total = dot(grad_both_all[:own_units], rows_all, (1, 0), BF16)
        down_total_ff = dot(act_all, grads_all, (1, 0), BF16)
        pairs = [(i, i ^ 1) for i in range(dp_size)]

        def pz(values):
            return lax.ppermute(values, "dp", pairs)

        def to_tile(total):
            kept = half_of(total, 1, row)
            fetched = px(half_of(total, 1, 1 - row))
            kept, fetched = pair(odd == 0, kept, pz(kept), 0), pair(odd == 0, fetched, pz(fetched), 0)
            return pair(first_x, kept, fetched, 0).astype(F32)

        up_grad_t, gate_grad_t, down_grad = (to_tile(g) for g in (up_total, gate_total, down_total_ff))
    else:

        def to_tile(part):
            total = lax.psum(part, "dp")
            return pair(first_x, half_of(total, 1, row), px(half_of(total, 1, 1 - row)), 0).astype(F32)

        up_grad_t, gate_grad_t, down_grad = (
            to_tile(dot(a, b, (1, 0), BF16))
            for a, b in (
                (grad_both[units:], normed_mid), (grad_both[:units], normed_mid), (activation, grad_down),
            )
        )

    out_part = dot(attended, grad_branch, (0, 0), BF16)
    out_grad = lax.psum(pair(first_x, half_of(out_part, 1, row), px(half_of(out_part, 1, 1 - row)), 0), "dp")
    up_part = dot(compressed, query_grad, (0, 0), BF16).reshape(QR, heads, SLOT)[:, :, : NOPE + RD]
    up_part = up_part.reshape(QR, query_columns)
    query_up_grad = lax.psum(pair(first_x, half_of(up_part, 0, row), px(half_of(up_part, 0, 1 - row)), 1), "dp")
    latent_part_grad = dot(latent, keyval_grad, (0, 0), BF16)
    latent_up_grad = lax.psum(pair(first_x, latent_part_grad, px(latent_part_grad), 1), "dp")
    normed_rows = jnp.concatenate([normed_half, py(normed_half)], 0)
    normed_rows = jnp.concatenate([normed_rows, pc(normed_rows)], 0)
    low_blocks = [latent_low[:, i * tile_width : (i + 1) * tile_width] for i in range(4)]
    low_rows = jnp.concatenate([low_blocks[0], py(low_blocks[1]), pc(low_blocks[2]), pyc(low_blocks[3])], 0)
    down_part = dot(low_rows, normed_rows, (0, 0), BF16)
    down_total = lax.psum(down_part, "dp").astype(F32)

    own_gains = jnp.concatenate([gain_mid_part, query_gain_part, latent_gain_part]).reshape(-1, SLOT)
    gain_totals = total_over(own_gains, ("core", "y", "x"), dp_size).reshape(-1)
    width = 2 * half_width
    return (
        output,
        input_gradient,
        gain_in_total,
        down_total[:query_tile].T,
        gain_totals[width : width + QR],
        query_up_grad.astype(F32),
        down_total[query_tile:].T,
        gain_totals[width + QR :],
        latent_up_grad.astype(F32),
        out_grad.astype(F32),
        lax.dynamic_slice_in_dim(gain_totals, row * half_width, half_width, 0),
        gate_grad_t.T,
        up_grad_t.T,
        down_grad,
    )


def solution(mesh):
    dp_size = mesh.shape["dp"]

    def program(*arguments):
        return per_device(dp_size, *arguments)

    return jax.shard_map(
        program,
        mesh=mesh,
        in_specs=(
            P(("dp", "col"), "row"),
            P(("dp", "col"), "row"),
            P("dp"),
            P("dp"),
            P("row"),
            P("row", "col"),
            P(),
            P("row", "col"),
            P("row", "col"),
            P(),
            P(None, "col"),
            P("col", "row"),
            P("row"),
            P("row", "col"),
            P("row", "col"),
            P("col", "row"),
        ),
        out_specs=(
            P(("dp", "col"), "row"),
            P(("dp", "col"), "row"),
            P("row"),
            P("row", "col"),
            P(),
            P("row", "col"),
            P("row", "col"),
            P(),
            P(None, "col"),
            P("col", "row"),
            P("row"),
            P("row", "col"),
            P("row", "col"),
            P("col", "row"),
        ),
        check_vma=False,
    )
```

```python
import math

import jax
import jax.numpy as jnp
from jax import lax
from jax.experimental import pallas as pl
from jax.experimental.pallas import tpu as pltpu
from jax.sharding import PartitionSpec as P

D = 2560
QR = 768
KVR = 256
NOPE = 64
RD = 32
VD = 64
SLOT = 128

EPSILON = 1e-05
RESIDUAL_SCALE = 1.4 / math.sqrt(62.0)
SCORE_SCALE = (NOPE + RD) ** (-0.5)
MASKED = -1000000000.0
F32 = jnp.float32
BF16 = jnp.bfloat16

OVER_X = ((0, 1), (1, 0))
OVER_CORE = ((0, 1), (1, 0), (2, 3), (3, 2))
OVER_Y = ((0, 2), (1, 3), (2, 0), (3, 1))
OVER_YCORE = ((0, 3), (1, 2), (2, 1), (3, 0))


def px(values):
    return lax.ppermute(values, "row", OVER_X)


def pc(values):
    return lax.ppermute(values, "col", OVER_CORE)


def py(values):
    return lax.ppermute(values, "col", OVER_Y)


def pyc(values):
    return lax.ppermute(values, "col", OVER_YCORE)


def dot(a, b, contract, out=F32):
    return lax.dot_general(a, b, ((contract[:1], contract[1:]), ((), ())), preferred_element_type=out)


def rows_at(values, start, length):
    return lax.dynamic_slice_in_dim(values, start, length, 0)


def pair(first_is_own, own, other, axis):
    return jnp.where(
        first_is_own,
        jnp.concatenate([own, other], axis),
        jnp.concatenate([other, own], axis),
    )


def together(*values):
    return lax.optimization_barrier(values)


def gather_near(own):
    return own, px(own), py(own)


def gather_far(own, from_x, from_y):
    half = own.shape[0] // 2
    return [own, from_x, from_y, py(from_x[:half]), px(from_y[half:])]


def gather_core(pieces):
    same_core = jnp.concatenate(pieces, 0)
    return jnp.concatenate([same_core, pc(same_core)], 0)


def gather_plane(own):
    return gather_core(gather_far(*gather_near(own)))


def scatter_core(partial):
    half = partial.shape[0] // 2
    return (partial[:half].astype(F32) + pc(partial[half:]).astype(F32)).astype(BF16)


def scatter_far(total):
    rows = total.shape[0] // 4
    half = rows // 2
    own, to_x, to_y, far = (total[i * rows : (i + 1) * rows] for i in range(4))
    return own, to_x, to_y, px(far[:half]), py(far[half:])


def scatter_near(own, to_x, to_y, for_y, for_x):
    half = for_y.shape[0]
    y_top = (to_y[:half].astype(F32) + for_y.astype(F32)).astype(BF16)
    x_low = (to_x[half:].astype(F32) + for_x.astype(F32)).astype(BF16)
    from_x = px(jnp.concatenate([to_x[:half], x_low], 0))
    from_y = py(jnp.concatenate([y_top, to_y[half:]], 0))
    return own.astype(F32) + from_x.astype(F32) + from_y.astype(F32)


def scatter_plane(partial):
    return scatter_near(*scatter_far(scatter_core(partial)))


def rms_norm(values, scaling):
    return values * lax.rsqrt(jnp.mean(values * values, axis=-1, keepdims=True) + EPSILON) * scaling


def rotate(values, cosine, sine_part):
    half_width = values.shape[-1] // 2
    first_half = values[..., :half_width]
    second_half = values[..., half_width:]
    return jnp.concatenate(
        [
            first_half * cosine - second_half * sine_part,
            second_half * cosine + first_half * sine_part,
        ],
        axis=-1,
    )


def turned(values, cosine, low_sine, high_sine):
    return (
        values * cosine
        + pltpu.roll(values, SLOT - RD // 2, 1) * low_sine
        + pltpu.roll(values, RD // 2, 1) * high_sine
    )


def allowed_bias(q_seq, q_block, k_seq, k_block):
    allowed = (q_seq == k_seq) & (k_block <= q_block)
    return jnp.where(allowed, 0.0, MASKED)


def attend_kernel(
    heads, comp, lat, rope, cosine, low_sine, high_sine, w_query, w_keyval, q_seq, q_block, k_seq, k_block,
    query_out, key_out, value_out, attended_out, lse_out,
):
    @pl.when(pl.program_id(0) == 0)
    def _():
        keyval = jnp.dot(lat[...], w_keyval[...], preferred_element_type=F32)
        lanes = lax.broadcasted_iota(jnp.int32, (lat.shape[0], SLOT), 1)
        for h in range(heads):
            part = keyval[:, h * SLOT : (h + 1) * SLOT]
            key_out[:, h * SLOT : (h + 1) * SLOT] = jnp.where(
                lanes < NOPE, part, rope[...].astype(F32)
            ).astype(BF16)
            value_out[:, h * VD : (h + 1) * VD] = part[:, NOPE:].astype(BF16)

    bias = allowed_bias(q_seq[...], q_block[...], k_seq[...], k_block[...])
    raw = jnp.dot(comp[...], w_query[...], preferred_element_type=F32)
    for h in range(heads):
        slot = slice(h * SLOT, (h + 1) * SLOT)
        query = turned(raw[:, slot], cosine[...], low_sine[...], high_sine[...]).astype(BF16)
        query_out[:, slot] = query
        scores = dot(query, key_out[:, slot], (1, 1)) * SCORE_SCALE + bias
        highest = jnp.max(scores, axis=1, keepdims=True)
        powers = jnp.exp(scores - highest)
        total = jnp.sum(powers, axis=1, keepdims=True)
        probs = (powers * (1.0 / total)).astype(BF16)
        result = jnp.dot(probs, value_out[:, h * VD : (h + 1) * VD], preferred_element_type=F32)
        attended_out[:, h * VD : (h + 1) * VD] = result.astype(BF16)
        lse_out[:, h : h + 1] = highest + jnp.log(total)


def attend_back_kernel(
    heads, query, key, value, lse, grad_out, cosine, low_sine, high_sine, q_seq, q_block, k_seq, k_block,
    query_grad, keyval_grad, rope_grad, key_total, value_total,
):
    step = pl.program_id(0)

    @pl.when(step == 0)
    def _():
        key_total[...] = jnp.zeros_like(key_total)
        value_total[...] = jnp.zeros_like(value_total)

    bias = allowed_bias(q_seq[...], q_block[...], k_seq[...], k_block[...])
    for h in range(heads):
        slot = slice(h * SLOT, (h + 1) * SLOT)
        narrow = slice(h * VD, (h + 1) * VD)
        scores = dot(query[:, slot], key[:, slot], (1, 1)) * SCORE_SCALE + bias
        probs = jnp.exp(scores - lse[:, h : h + 1])
        grad_probs = dot(grad_out[:, narrow], value[:, narrow], (1, 1))
        inner = jnp.sum(probs * grad_probs, axis=1, keepdims=True)
        grad_dots = (probs * (grad_probs - inner) * SCORE_SCALE).astype(BF16)
        back = jnp.dot(grad_dots, key[:, slot], preferred_element_type=F32)
        query_grad[:, slot] = turned(back, cosine[...], -low_sine[...], -high_sine[...]).astype(BF16)
        key_total[:, slot] += dot(grad_dots, query[:, slot], (0, 0))
        value_total[:, narrow] += dot(probs.astype(BF16), grad_out[:, narrow], (0, 0))

    @pl.when(step == pl.num_programs(0) - 1)
    def _():
        rope_total = jnp.zeros((key.shape[0], SLOT), F32)
        for h in range(heads):
            part = key_total[:, h * SLOT : (h + 1) * SLOT]
            rope_total = rope_total + part
            keyval_grad[:, h * SLOT : h * SLOT + NOPE] = part[:, :NOPE].astype(BF16)
            keyval_grad[:, h * SLOT + NOPE : (h + 1) * SLOT] = value_total[:, h * VD : (h + 1) * VD].astype(BF16)
        lanes = lax.broadcasted_iota(jnp.int32, rope_total.shape, 1)
        rope_grad[...] = jnp.where(lanes >= NOPE, rope_total, 0.0).astype(BF16)


def row_tile(rows, width):
    return pl.BlockSpec((rows, width), lambda i: (i, 0))


def whole(shape):
    return pl.BlockSpec(shape, lambda i: (0, 0))


def attend(latents, turns, w_query, w_keyval, marks, heads, tile):
    rows = latents.shape[0]
    column = row_tile(tile, 1)
    line = whole((1, rows))
    return pl.pallas_call(
        lambda *refs: attend_kernel(heads, *refs),
        grid=(rows // tile,),
        in_specs=[
            row_tile(tile, QR), pl.BlockSpec((rows, KVR), lambda i: (0, QR // KVR)),
            pl.BlockSpec((rows, SLOT), lambda i: (0, (QR + KVR) // SLOT)),
            row_tile(tile, SLOT), row_tile(tile, SLOT), row_tile(tile, SLOT),
            whole(w_query.shape), whole(w_keyval.shape), column, column, line, line,
        ],
        out_specs=[
            row_tile(tile, heads * SLOT), whole((rows, heads * SLOT)), whole((rows, heads * VD)),
            row_tile(tile, heads * VD), row_tile(tile, 8),
        ],
        out_shape=[
            jax.ShapeDtypeStruct((rows, heads * SLOT), BF16),
            jax.ShapeDtypeStruct((rows, heads * SLOT), BF16),
            jax.ShapeDtypeStruct((rows, heads * VD), BF16),
            jax.ShapeDtypeStruct((rows, heads * VD), BF16),
            jax.ShapeDtypeStruct((rows, 8), F32),
        ],
        compiler_params=pltpu.CompilerParams(vmem_limit_bytes=48 << 20),
        cost_estimate=pl.CostEstimate(
            flops=2 * rows * heads * (rows * 2 * SLOT + QR * SLOT), bytes_accessed=8 << 20,
            transcendentals=heads * rows * rows,
        ),
        name="attend",
    )(latents, latents, latents, *turns, w_query, w_keyval, *marks)


def attend_back(query, key, value, lse, grad_out, turns, marks, heads, tile):
    rows = query.shape[0]
    column = row_tile(tile, 1)
    line = whole((1, rows))
    return pl.pallas_call(
        lambda *refs: attend_back_kernel(heads, *refs),
        grid=(rows // tile,),
        in_specs=[
            row_tile(tile, heads * SLOT), whole((rows, heads * SLOT)), whole((rows, heads * VD)),
            row_tile(tile, 8), row_tile(tile, heads * VD),
            row_tile(tile, SLOT), row_tile(tile, SLOT), row_tile(tile, SLOT), column, column, line, line,
        ],
        out_specs=[
            row_tile(tile, heads * SLOT), whole((rows, heads * SLOT)), whole((rows, SLOT)),
        ],
        out_shape=[
            jax.ShapeDtypeStruct((rows, heads * SLOT), BF16),
            jax.ShapeDtypeStruct((rows, heads * SLOT), BF16),
            jax.ShapeDtypeStruct((rows, SLOT), BF16),
        ],
        scratch_shapes=[pltpu.VMEM((rows, heads * SLOT), F32), pltpu.VMEM((rows, heads * VD), F32)],
        compiler_params=pltpu.CompilerParams(vmem_limit_bytes=48 << 20),
        cost_estimate=pl.CostEstimate(
            flops=2 * rows * heads * rows * 5 * SLOT, bytes_accessed=8 << 20, transcendentals=heads * rows * rows,
        ),
        name="attend_back",
    )(query, key, value, lse, grad_out, *turns, *marks)


def activate(gate, up, grad_act):
    sigmoid_gate = jax.nn.sigmoid(gate)
    swish = gate * sigmoid_gate
    grad_gate = grad_act * up * sigmoid_gate * (1.0 + gate * (1.0 - sigmoid_gate))
    return (swish * up).astype(BF16), grad_gate.astype(BF16), (grad_act * swish).astype(BF16)


def per_device(
    dp_size, hidden, cotangent, sequence_index, block_index, attention_gain, query_down, query_gain, query_up,
    latent_down, latent_gain, latent_up, attention_out, feedforward_gain, gate_weight, up_weight, down_weight,
):
    dp_place, row, col = lax.axis_index("dp"), lax.axis_index("row"), lax.axis_index("col")
    first_x = row == 0
    token_rows = hidden.shape[0]
    own_rows = token_rows // 2
    group_rows = sequence_index.shape[0]
    half_width = hidden.shape[1]
    heads = query_up.shape[1] // (NOPE + RD) // 2
    units = gate_weight.shape[1] // 2
    tile = group_rows // 4
    shard_order = [(a, b) for b in (0, 2) for a in (0, 1)] + [(a, b) for b in (1, 3) for a in (0, 1)]
    places = [((col ^ b) * 2 + (row ^ a)) for a, b in shard_order]

    def half_of(values, axis, which):
        length = values.shape[axis] // 2
        return lax.dynamic_slice_in_dim(values, which * length, length, axis)

    middle_plane = (dp_place == 1) | (dp_place == 2)

    def add(a, b):
        return (a.astype(F32) + b.astype(F32)).astype(BF16)

    def inward(part):
        return part, lax.ppermute(part, "dp", ((0, 1), (3, 2)))

    def across(part, arrived):
        near = add(part, arrived)
        return near, lax.ppermute(near, "dp", ((1, 2), (2, 1)))

    def outward(near, far):
        total = add(near, far)
        return total, lax.ppermute(total, "dp", ((1, 0), (2, 3)))

    def settled(total, back):
        return jnp.where(middle_plane, total, back)

    pairs = [(i, i ^ 1) for i in range(dp_size)]
    odd = dp_place % 2
    barrier = lax.optimization_barrier

    gain_in = attention_gain.astype(F32)
    hidden_wide = hidden.astype(F32)
    squares = jnp.sum(hidden_wide * hidden_wide, axis=1)[None, :]
    inverse_half = lax.rsqrt((squares + px(squares))[0] / (2 * half_width) + EPSILON)
    inverse_in = half_of(inverse_half, 0, row)
    scaled_in = hidden_wide * inverse_half[:, None]
    normed_half = (scaled_in * gain_in[None, :]).astype(BF16)

    by_factors = dp_size == 4
    every = ("dp", "row", "col")

    latent_tile = jnp.concatenate([query_down.T, latent_down.T], 0)
    tile_width = latent_tile.shape[0]
    near_tiles = jnp.concatenate([latent_tile, py(latent_tile)], 0)

    tiles = [gate_weight.T, up_weight.T, down_weight]
    count = units // dp_size
    wanted = [rows_at(t, (1 - row) * units + dp_place * count, count) for t in tiles]
    fetched = px(jnp.concatenate(wanted, 0))
    latent_weights = jnp.concatenate([near_tiles, pc(near_tiles)], 0)
    query_columns = query_up.shape[1] // 2
    w_keyval = half_of(latent_up, 1, row)

    second = jnp.sum((sequence_index == sequence_index[0]).astype(jnp.int32))
    inverse_rate = -2.0 * math.log(10000.0) / RD

    def in_order(values):
        return jnp.concatenate([rows_at(values, place * own_rows, own_rows) for place in places], 0)

    seq_all, block_all = in_order(sequence_index), in_order(block_index)
    index_all = in_order(jnp.arange(group_rows, dtype=jnp.int32))
    position = (index_all - jnp.where(seq_all == sequence_index[0], 0, second)).astype(F32)
    lane = jnp.arange(SLOT, dtype=jnp.int32)
    turning = (lane >= NOPE) & (lane < NOPE + RD)
    rate = jnp.exp(((lane - NOPE) % (RD // 2)).astype(F32) * inverse_rate)
    angle = jnp.where(turning, rate, 0.0)[None, :] * position[:, None]
    cosine, sine = jnp.cos(angle), jnp.sin(angle)
    low_sine = jnp.where(lane < NOPE + RD // 2, -sine, 0.0)
    high_sine = jnp.where(lane >= NOPE + RD // 2, sine, 0.0)
    turns = (cosine, low_sine, high_sine)
    marks = (seq_all[:, None], block_all[:, None], seq_all[None, :], block_all[None, :])
    own_cosine = cosine[:own_rows, NOPE : NOPE + RD // 2]
    own_sine = sine[:own_rows, NOPE : NOPE + RD // 2]

    latent_part = dot(normed_half, latent_weights, (1, 1))
    latent_other, query_other = together(half_of(latent_part, 0, 1 - row), half_of(query_up, 1, 1 - row))
    latent_other, query_other = px(latent_other), px(query_other)
    normed_y = py(normed_half)
    latent_raw = half_of(latent_part, 0, row) + latent_other
    latent_raw, fetched = together(latent_raw, fetched)
    others = lax.all_gather(fetched, "dp", axis=0, tiled=True)

    def in_place(values):
        blocks = [values[:, i * tile_width : (i + 1) * tile_width] for i in range(4)]
        core, high = (col % 2) == 1, (col // 2) == 1
        b0, b2, b1, b3 = blocks
        c0, c1 = jnp.where(core, b1, b0), jnp.where(core, b0, b1)
        c2, c3 = jnp.where(core, b3, b2), jnp.where(core, b2, b3)
        return (
            jnp.where(high, c2, c0), jnp.where(high, c3, c1), jnp.where(high, c0, c2), jnp.where(high, c1, c3),
        )

    blocks = in_place(latent_raw)
    query_tile = query_down.shape[1]
    query_latent = jnp.concatenate([b[:, :query_tile] for b in blocks], 1)
    kv_latent = jnp.concatenate([b[:, query_tile:] for b in blocks], 1)

    def latent_norms(query_values, key_values, query_scaling, key_scaling):
        return (
            rms_norm(query_values, query_scaling),
            rms_norm(key_values[:, :KVR], key_scaling),
            rotate(key_values[:, KVR:], own_cosine, own_sine),
        )

    own_latents, latent_back = jax.vjp(
        latent_norms, query_latent, kv_latent, query_gain.astype(F32), latent_gain.astype(F32)
    )
    side = ((0, 0), (NOPE, SLOT - NOPE - RD))
    latents_near = gather_near(jnp.concatenate([*own_latents[:2], jnp.pad(own_latents[2], side)], 1).astype(BF16))
    *latents_near, query_other = together(*latents_near, query_other)
    w_query = pair(first_x, half_of(query_up, 1, row), query_other, 0)
    w_query = jnp.pad(w_query.reshape(QR, heads, NOPE + RD), ((0, 0), (0, 0), (0, SLOT - NOPE - RD)))
    w_query = w_query.reshape(QR, heads * SLOT)
    latents = gather_core(gather_far(*latents_near))
    latents, w_query, out_late, hidden_late, cotangent_late, gain_late = together(
        latents, w_query, half_of(attention_out, 0, 1 - row), half_of(hidden, 0, 1 - row),
        half_of(cotangent, 0, 1 - row), feedforward_gain,
    )
    gain_mid = pair(first_x, feedforward_gain, px(gain_late), 0).astype(F32)
    out_other, hidden_other, cotangent_other = px(out_late), px(hidden_late), px(cotangent_late)
    compressed, latent = latents[:, :QR], latents[:, QR : QR + KVR]
    query, key, value, attended, lse = attend(
        latents, turns, w_query, w_keyval, marks, heads, tile
    )

    attended, out_other, hidden_other, cotangent_other, normed_y = together(
        attended, out_other, hidden_other, cotangent_other, normed_y
    )
    incoming = pair(first_x, half_of(cotangent, 0, row), cotangent_other, 1).astype(F32)
    grad_down_own = (RESIDUAL_SCALE * incoming).astype(BF16)
    normed_rows = jnp.concatenate([normed_half, normed_y], 0)
    w_out = pair(first_x, half_of(attention_out, 0, row), out_other, 1)
    stream = pair(first_x, half_of(hidden, 0, row), hidden_other, 1).astype(F32)
    branch = scatter_core(dot(attended, w_out, (1, 0), BF16))
    middle = stream + RESIDUAL_SCALE * scatter_near(*scatter_far(branch))
    inverse_mid = lax.rsqrt(jnp.mean(middle * middle, axis=1, keepdims=True) + EPSILON)
    scaled_mid = middle * inverse_mid
    normed_mid_own = (scaled_mid * gain_mid[None, :]).astype(BF16)

    def assembled(weights, start, which):
        own = rows_at(tiles[which], row * units, units)
        weights = lax.dynamic_update_slice(weights, own, (start, row * half_width))
        for k in range(dp_size):
            other = others[(3 * k + which) * count : (3 * k + which + 1) * count]
            weights = lax.dynamic_update_slice(weights, other, (start + k * count, (1 - row) * half_width))
        return weights

    if by_factors:
        rows_all = lax.all_gather(normed_mid_own, every, axis=0, tiled=True)
    normed_near = gather_near(normed_mid_own)
    *normed_near, others, normed_rows, grad_down_own = together(*normed_near, others, normed_rows, grad_down_own)
    if by_factors:
        grads_all = lax.all_gather(grad_down_own, every, axis=0, tiled=True)
    normed_far = gather_far(*normed_near)
    grad_down_near = gather_near(grad_down_own)
    gate_up = jnp.zeros((2 * units, 2 * half_width), BF16)
    gate_up = assembled(assembled(gate_up, 0, 0), units, 1)
    down = assembled(jnp.zeros((units, 2 * half_width), BF16), 0, 2)
    normed_mid = gather_core(normed_far)
    normed_mid, *grad_down_near = together(normed_mid, *grad_down_near)
    grad_down_far = gather_far(*grad_down_near)
    normed_rows = jnp.concatenate([normed_rows, pc(normed_rows)], 0)
    both, *grad_down_far = together(dot(gate_up, normed_mid, (1, 1)), *grad_down_far)
    grad_down = gather_core(grad_down_far)
    grad_act = dot(down, grad_down, (1, 1))
    activation, grad_gate, grad_up = activate(both[:units], both[units:], grad_act)
    activation, grad_both = together(activation, jnp.concatenate([grad_gate, grad_up], 0))

    mid_total = scatter_core(dot(grad_both, gate_up, (0, 0), BF16))
    mid_total, activation = together(mid_total, activation)
    mid_steps = scatter_far(mid_total)
    upstream_mid = scatter_near(*mid_steps)
    weighted = upstream_mid * gain_mid[None, :]
    mean_inner = jnp.mean(weighted * scaled_mid, axis=1, keepdims=True)
    gain_mid_part = jnp.sum(upstream_mid * scaled_mid, axis=0)
    grad_middle = incoming + inverse_mid * (weighted - scaled_mid * mean_inner)
    branch_near = gather_near((RESIDUAL_SCALE * grad_middle).astype(BF16))
    *branch_near, activation_late = together(*branch_near, activation)
    branch_far = gather_far(*branch_near)
    output_part = dot(activation_late, down, (0, 0), BF16)
    *branch_far, output_part = together(*branch_far, output_part)
    grad_branch = gather_core(branch_far)

    grad_attended = dot(grad_branch, w_out, (1, 1), BF16)
    out_part = dot(attended, grad_branch, (0, 0), BF16)
    grad_attended, out_part = together(grad_attended, out_part)
    out_other = px(half_of(out_part, 1, 1 - row))
    query_grad, keyval_grad, rope_grad = attend_back(
        query, key, value, lse, grad_attended, turns, marks, heads, tile
    )
    query_grad, keyval_grad, rope_grad, out_other = together(query_grad, keyval_grad, rope_grad, out_other)
    out_part = pair(first_x, half_of(out_part, 1, row), out_other, 0)
    latent_grad_part = jnp.concatenate(
        [
            dot(query_grad, w_query, (1, 1), BF16),
            dot(keyval_grad, w_keyval, (1, 1), BF16),
            rope_grad,
        ],
        1,
    )
    latent_steps = scatter_far(scatter_core(latent_grad_part))
    if by_factors:
        *latent_steps, rows_all = together(*latent_steps, rows_all)
        gate_all = dot(gate_up[:units], rows_all, (1, 1))
    latent_steps = list(latent_steps)
    latent_grad = scatter_near(*latent_steps)
    if by_factors:
        latent_grad, gate_all, output_part = together(latent_grad, gate_all, output_part)
    query_latent_grad, kv_latent_grad, query_gain_part, latent_gain_part = latent_back(
        (latent_grad[:, :QR], latent_grad[:, QR : QR + KVR], latent_grad[:, QR + KVR + NOPE : QR + KVR + NOPE + RD])
    )
    kv_tile = latent_down.shape[1]
    query_low, kv_low = query_latent_grad.astype(BF16), kv_latent_grad.astype(BF16)
    inner_in = (
        jnp.sum(query_low.astype(F32) * query_latent, axis=1) + jnp.sum(kv_low.astype(F32) * kv_latent, axis=1)
    ) / D
    in_blocks = jnp.concatenate(
        [
            part
            for i in (0, 2, 1, 3)
            for part in (
                query_low[:, i * query_tile : (i + 1) * query_tile],
                kv_low[:, i * kv_tile : (i + 1) * kv_tile],
            )
        ],
        1,
    )
    g0, g1, g2, g3 = in_place(in_blocks)
    latent_low = jnp.concatenate([g0, g2, g1, g3], 1)
    low_other, inner_other = px(latent_low), px(inner_in[None, :])[0]
    if by_factors:
        out_1 = inward(out_part)
        up_all = dot(gate_up[units:], rows_all, (1, 1))
        low_other, up_all, out_1 = barrier((low_other, up_all, out_1))
    latent_low = pair(first_x, latent_low, low_other, 0)
    inner_half = pair(first_x, inner_in, inner_other, 0)
    grad_normed = dot(latent_low, latent_weights, (1, 0))
    grad_middle_half = pair(
        first_x,
        half_of(grad_middle, 1, row),
        px(half_of(grad_middle, 1, 1 - row).astype(BF16)).astype(F32),
        0,
    )
    grad_in = inverse_half[:, None] * (grad_normed * gain_in[None, :] - scaled_in * inner_half[:, None])
    input_gradient = (grad_middle_half + grad_in).astype(BF16)
    gain_in_part = jnp.sum(grad_normed * scaled_in, axis=0)

    output_own = (middle + RESIDUAL_SCALE * scatter_plane(output_part)).astype(BF16)
    output = pair(first_x, half_of(output_own, 1, row), px(half_of(output_own, 1, 1 - row)), 0)

    up_part = dot(compressed, query_grad, (0, 0), BF16).reshape(QR, heads, SLOT)[:, :, : NOPE + RD]
    up_part = up_part.reshape(QR, query_columns)
    up_part = pair(first_x, half_of(up_part, 0, row), px(half_of(up_part, 0, 1 - row)), 1)
    latent_up_part = dot(latent, keyval_grad, (0, 0), BF16)
    latent_up_part = pair(first_x, latent_up_part, px(latent_up_part), 1)
    low_blocks = [latent_low[:, i * tile_width : (i + 1) * tile_width] for i in range(4)]
    low_rows = jnp.concatenate([low_blocks[0], py(low_blocks[1]), pc(low_blocks[2]), pyc(low_blocks[3])], 0)
    latent_down_part = dot(low_rows, normed_rows, (0, 0), BF16)

    gains = jnp.concatenate([gain_in_part, gain_mid_part, query_gain_part, latent_gain_part]).reshape(-1, SLOT)
    gains = gains + pc(gains)
    gains = gains + py(gains)
    own_gains = half_width // SLOT
    gains = jnp.concatenate([gains[:own_gains], gains[own_gains:] + px(gains[own_gains:])], 0).reshape(-1)
    gain_count = gains.shape[0]
    gains = jnp.pad(gains, (0, -gain_count % half_width)).reshape(-1, half_width).astype(BF16)
    latent_down_part = jnp.concatenate([latent_down_part, gains], 0)
    if by_factors:
        input_gradient, grads_all, up_part = barrier((input_gradient, grads_all, up_part))
        out_2, up_1 = across(*out_1), inward(up_part)
        grad_act_all = dot(down, grads_all, (1, 1))
        gate_all, up_all, grad_act_all, out_2, up_1, latent_up_part, output = barrier(
            (gate_all, up_all, grad_act_all, out_2, up_1, latent_up_part, output)
        )
        out_3, up_2, latent_1 = outward(*out_2), across(*up_1), inward(latent_up_part)
        act_all, grad_gate_all, grad_up_all = activate(gate_all, up_all, grad_act_all)
        act_all, grad_gate_all, grad_up_all, up_2, latent_1, latent_down_part = barrier(
            (act_all, grad_gate_all, grad_up_all, up_2, latent_1, latent_down_part)
        )
        up_3, latent_2, down_1 = outward(*up_2), across(*latent_1), inward(latent_down_part)
        own_units = units // 2

        def to_send(total):
            return rows_at(half_of(total, 1, 1 - row), odd * own_units, own_units)

        def pz(values):
            return lax.ppermute(values, "dp", pairs)

        up_total = dot(grad_up_all, rows_all, (1, 0), BF16)
        up_total, grad_gate_all, latent_2, down_1 = barrier((up_total, grad_gate_all, latent_2, down_1))
        latent_3, down_2 = outward(*latent_2), across(*down_1)
        up_other = px(to_send(up_total))
        gate_total = dot(grad_gate_all, rows_all, (1, 0), BF16)
        gate_total, act_all, down_2, up_other = barrier((gate_total, act_all, down_2, up_other))
        down_3 = outward(*down_2)
        up_far, gate_other = pz(up_other), px(to_send(gate_total))
        down_ff = dot(act_all, grads_all, (1, 0), BF16)
        down_ff, up_far, gate_other = barrier((down_ff, up_far, gate_other))
        gate_far, down_other = pz(gate_other), px(to_send(down_ff))
        unit_grads = [up_total, gate_total, down_ff]
        up_other, gate_other, down_other = (
            pair(odd == 0, other, far, 0)
            for other, far in ((up_other, up_far), (gate_other, gate_far), (down_other, pz(down_other)))
        )
        unit_others = [up_other, gate_other, down_other]
        out_grad, query_up_grad = settled(*out_3), settled(*up_3)
        latent_up_grad, down_total = settled(*latent_3), settled(*down_3)
    else:
        unit_grads = [
            lax.psum(dot(a, b, (1, 0), BF16), "dp")
            for a, b in (
                (grad_both[units:], normed_mid), (grad_both[:units], normed_mid), (activation, grad_down),
            )
        ]
        unit_others = [px(half_of(total, 1, 1 - row)) for total in unit_grads]
        out_grad, query_up_grad, latent_up_grad, down_total = (
            lax.psum(part, "dp") for part in (out_part, up_part, latent_up_part, latent_down_part)
        )
    up_grad_t, gate_grad_t, down_grad = (
        pair(first_x, half_of(total, 1, row), other, 0).astype(F32) for total, other in zip(unit_grads, unit_others)
    )
    down_total = down_total.astype(F32)
    gain_totals = down_total[tile_width:].reshape(-1)
    gain_in_total, gain_totals = gain_totals[:half_width], gain_totals[half_width:gain_count]
    width = 2 * half_width
    return (
        output,
        input_gradient,
        gain_in_total,
        down_total[:query_tile].T,
        gain_totals[width : width + QR],
        query_up_grad.astype(F32),
        down_total[query_tile:tile_width].T,
        gain_totals[width + QR :],
        latent_up_grad.astype(F32),
        out_grad.astype(F32),
        lax.dynamic_slice_in_dim(gain_totals, row * half_width, half_width, 0),
        gate_grad_t.T,
        up_grad_t.T,
        down_grad,
    )


def solution(mesh):
    dp_size = mesh.shape["dp"]

    def program(*arguments):
        return per_device(dp_size, *arguments)

    return jax.shard_map(
        program,
        mesh=mesh,
        in_specs=(
            P(("dp", "col"), "row"),
            P(("dp", "col"), "row"),
            P("dp"),
            P("dp"),
            P("row"),
            P("row", "col"),
            P(),
            P("row", "col"),
            P("row", "col"),
            P(),
            P(None, "col"),
            P("col", "row"),
            P("row"),
            P("row", "col"),
            P("row", "col"),
            P("col", "row"),
        ),
        out_specs=(
            P(("dp", "col"), "row"),
            P(("dp", "col"), "row"),
            P("row"),
            P("row", "col"),
            P(),
            P("row", "col"),
            P("row", "col"),
            P(),
            P(None, "col"),
            P("col", "row"),
            P("row"),
            P("row", "col"),
            P("row", "col"),
            P("col", "row"),
        ),
        check_vma=False,
    )
```

```python
import math

import jax
import jax.numpy as jnp
from jax import lax
from jax.experimental import pallas as pl
from jax.experimental.pallas import tpu as pltpu
from jax.sharding import PartitionSpec as P

D = 2560
QR = 768
KVR = 256
NOPE = 64
RD = 32
VD = 64
SLOT = 128

EPSILON = 1e-05
RESIDUAL_SCALE = 1.4 / math.sqrt(62.0)
SCORE_SCALE = (NOPE + RD) ** (-0.5)
MASKED = -1000000000.0
F32 = jnp.float32
BF16 = jnp.bfloat16

OVER_X = ((0, 1), (1, 0))
OVER_CORE = ((0, 1), (1, 0), (2, 3), (3, 2))
OVER_Y = ((0, 2), (1, 3), (2, 0), (3, 1))
OVER_YCORE = ((0, 3), (1, 2), (2, 1), (3, 0))


def px(values):
    return lax.ppermute(values, "row", OVER_X)


def pc(values):
    return lax.ppermute(values, "col", OVER_CORE)


def py(values):
    return lax.ppermute(values, "col", OVER_Y)


def pyc(values):
    return lax.ppermute(values, "col", OVER_YCORE)


def dot(a, b, contract, out=F32):
    return lax.dot_general(a, b, ((contract[:1], contract[1:]), ((), ())), preferred_element_type=out)


def rows_at(values, start, length):
    return lax.dynamic_slice_in_dim(values, start, length, 0)


def pair(first_is_own, own, other, axis):
    return jnp.where(
        first_is_own,
        jnp.concatenate([own, other], axis),
        jnp.concatenate([other, own], axis),
    )


def together(*values):
    return lax.optimization_barrier(values)


def gather_near(own):
    return own, px(own), py(own)


def gather_far(own, from_x, from_y):
    half = own.shape[0] // 2
    return [own, from_x, from_y, py(from_x[:half]), px(from_y[half:])]


def gather_core(pieces):
    same_core = jnp.concatenate(pieces, 0)
    return jnp.concatenate([same_core, pc(same_core)], 0)


def gather_plane(own):
    return gather_core(gather_far(*gather_near(own)))


def scatter_core(partial):
    half = partial.shape[0] // 2
    return (partial[:half].astype(F32) + pc(partial[half:]).astype(F32)).astype(BF16)


def scatter_far(total):
    rows = total.shape[0] // 4
    half = rows // 2
    own, to_x, to_y, far = (total[i * rows : (i + 1) * rows] for i in range(4))
    return own, to_x, to_y, px(far[:half]), py(far[half:])


def scatter_near(own, to_x, to_y, for_y, for_x):
    half = for_y.shape[0]
    y_top = (to_y[:half].astype(F32) + for_y.astype(F32)).astype(BF16)
    x_low = (to_x[half:].astype(F32) + for_x.astype(F32)).astype(BF16)
    from_x = px(jnp.concatenate([to_x[:half], x_low], 0))
    from_y = py(jnp.concatenate([y_top, to_y[half:]], 0))
    return own.astype(F32) + from_x.astype(F32) + from_y.astype(F32)


def scatter_plane(partial):
    return scatter_near(*scatter_far(scatter_core(partial)))


def rms_norm(values, scaling):
    return values * lax.rsqrt(jnp.mean(values * values, axis=-1, keepdims=True) + EPSILON) * scaling


def rotate(values, cosine, sine_part):
    half_width = values.shape[-1] // 2
    first_half = values[..., :half_width]
    second_half = values[..., half_width:]
    return jnp.concatenate(
        [
            first_half * cosine - second_half * sine_part,
            second_half * cosine + first_half * sine_part,
        ],
        axis=-1,
    )


def turned(values, cosine, low_sine, high_sine):
    return (
        values * cosine
        + pltpu.roll(values, SLOT - RD // 2, 1) * low_sine
        + pltpu.roll(values, RD // 2, 1) * high_sine
    )


def allowed_bias(q_seq, q_block, k_seq, k_block):
    allowed = (q_seq == k_seq) & (k_block <= q_block)
    return jnp.where(allowed, 0.0, MASKED)


def attend_kernel(
    heads, comp, lat, rope, cosine, low_sine, high_sine, w_query, w_keyval, q_seq, q_block, k_seq, k_block,
    query_out, key_out, value_out, attended_out, lse_out,
):
    @pl.when(pl.program_id(0) == 0)
    def _():
        keyval = jnp.dot(lat[...], w_keyval[...], preferred_element_type=F32)
        lanes = lax.broadcasted_iota(jnp.int32, (lat.shape[0], SLOT), 1)
        for h in range(heads):
            part = keyval[:, h * SLOT : (h + 1) * SLOT]
            key_out[:, h * SLOT : (h + 1) * SLOT] = jnp.where(
                lanes < NOPE, part, rope[...].astype(F32)
            ).astype(BF16)
            value_out[:, h * VD : (h + 1) * VD] = part[:, NOPE:].astype(BF16)

    bias = allowed_bias(q_seq[...], q_block[...], k_seq[...], k_block[...])
    raw = jnp.dot(comp[...], w_query[...], preferred_element_type=F32)
    for h in range(heads):
        slot = slice(h * SLOT, (h + 1) * SLOT)
        query = turned(raw[:, slot], cosine[...], low_sine[...], high_sine[...]).astype(BF16)
        query_out[:, slot] = query
        scores = dot(query, key_out[:, slot], (1, 1)) * SCORE_SCALE + bias
        highest = jnp.max(scores, axis=1, keepdims=True)
        powers = jnp.exp(scores - highest)
        total = jnp.sum(powers, axis=1, keepdims=True)
        probs = (powers * (1.0 / total)).astype(BF16)
        result = jnp.dot(probs, value_out[:, h * VD : (h + 1) * VD], preferred_element_type=F32)
        attended_out[:, h * VD : (h + 1) * VD] = result.astype(BF16)
        lse_out[:, h : h + 1] = highest + jnp.log(total)


def attend_back_kernel(
    heads, query, key, value, lse, grad_out, cosine, low_sine, high_sine, q_seq, q_block, k_seq, k_block,
    query_grad, keyval_grad, rope_grad, key_total, value_total,
):
    step = pl.program_id(0)

    @pl.when(step == 0)
    def _():
        key_total[...] = jnp.zeros_like(key_total)
        value_total[...] = jnp.zeros_like(value_total)

    bias = allowed_bias(q_seq[...], q_block[...], k_seq[...], k_block[...])
    for h in range(heads):
        slot = slice(h * SLOT, (h + 1) * SLOT)
        narrow = slice(h * VD, (h + 1) * VD)
        scores = dot(query[:, slot], key[:, slot], (1, 1)) * SCORE_SCALE + bias
        probs = jnp.exp(scores - lse[:, h : h + 1])
        grad_probs = dot(grad_out[:, narrow], value[:, narrow], (1, 1))
        inner = jnp.sum(probs * grad_probs, axis=1, keepdims=True)
        grad_dots = (probs * (grad_probs - inner) * SCORE_SCALE).astype(BF16)
        back = jnp.dot(grad_dots, key[:, slot], preferred_element_type=F32)
        query_grad[:, slot] = turned(back, cosine[...], -low_sine[...], -high_sine[...]).astype(BF16)
        key_total[:, slot] += dot(grad_dots, query[:, slot], (0, 0))
        value_total[:, narrow] += dot(probs.astype(BF16), grad_out[:, narrow], (0, 0))

    @pl.when(step == pl.num_programs(0) - 1)
    def _():
        rope_total = jnp.zeros((key.shape[0], SLOT), F32)
        for h in range(heads):
            part = key_total[:, h * SLOT : (h + 1) * SLOT]
            rope_total = rope_total + part
            keyval_grad[:, h * SLOT : h * SLOT + NOPE] = part[:, :NOPE].astype(BF16)
            keyval_grad[:, h * SLOT + NOPE : (h + 1) * SLOT] = value_total[:, h * VD : (h + 1) * VD].astype(BF16)
        lanes = lax.broadcasted_iota(jnp.int32, rope_total.shape, 1)
        rope_grad[...] = jnp.where(lanes >= NOPE, rope_total, 0.0).astype(BF16)


def row_tile(rows, width):
    return pl.BlockSpec((rows, width), lambda i: (i, 0))


def whole(shape):
    return pl.BlockSpec(shape, lambda i: (0, 0))


def attend(latents, turns, w_query, w_keyval, marks, heads, tile):
    rows = latents.shape[0]
    column = row_tile(tile, 1)
    line = whole((1, rows))
    return pl.pallas_call(
        lambda *refs: attend_kernel(heads, *refs),
        grid=(rows // tile,),
        in_specs=[
            row_tile(tile, QR), pl.BlockSpec((rows, KVR), lambda i: (0, QR // KVR)),
            pl.BlockSpec((rows, SLOT), lambda i: (0, (QR + KVR) // SLOT)),
            row_tile(tile, SLOT), row_tile(tile, SLOT), row_tile(tile, SLOT),
            whole(w_query.shape), whole(w_keyval.shape), column, column, line, line,
        ],
        out_specs=[
            row_tile(tile, heads * SLOT), whole((rows, heads * SLOT)), whole((rows, heads * VD)),
            row_tile(tile, heads * VD), row_tile(tile, 8),
        ],
        out_shape=[
            jax.ShapeDtypeStruct((rows, heads * SLOT), BF16),
            jax.ShapeDtypeStruct((rows, heads * SLOT), BF16),
            jax.ShapeDtypeStruct((rows, heads * VD), BF16),
            jax.ShapeDtypeStruct((rows, heads * VD), BF16),
            jax.ShapeDtypeStruct((rows, 8), F32),
        ],
        compiler_params=pltpu.CompilerParams(vmem_limit_bytes=48 << 20),
        cost_estimate=pl.CostEstimate(
            flops=2 * rows * heads * (rows * 2 * SLOT + QR * SLOT), bytes_accessed=8 << 20,
            transcendentals=heads * rows * rows,
        ),
        name="attend",
    )(latents, latents, latents, *turns, w_query, w_keyval, *marks)


def attend_back(query, key, value, lse, grad_out, turns, marks, heads, tile):
    rows = query.shape[0]
    column = row_tile(tile, 1)
    line = whole((1, rows))
    return pl.pallas_call(
        lambda *refs: attend_back_kernel(heads, *refs),
        grid=(rows // tile,),
        in_specs=[
            row_tile(tile, heads * SLOT), whole((rows, heads * SLOT)), whole((rows, heads * VD)),
            row_tile(tile, 8), row_tile(tile, heads * VD),
            row_tile(tile, SLOT), row_tile(tile, SLOT), row_tile(tile, SLOT), column, column, line, line,
        ],
        out_specs=[
            row_tile(tile, heads * SLOT), whole((rows, heads * SLOT)), whole((rows, SLOT)),
        ],
        out_shape=[
            jax.ShapeDtypeStruct((rows, heads * SLOT), BF16),
            jax.ShapeDtypeStruct((rows, heads * SLOT), BF16),
            jax.ShapeDtypeStruct((rows, SLOT), BF16),
        ],
        scratch_shapes=[pltpu.VMEM((rows, heads * SLOT), F32), pltpu.VMEM((rows, heads * VD), F32)],
        compiler_params=pltpu.CompilerParams(vmem_limit_bytes=48 << 20),
        cost_estimate=pl.CostEstimate(
            flops=2 * rows * heads * rows * 5 * SLOT, bytes_accessed=8 << 20, transcendentals=heads * rows * rows,
        ),
        name="attend_back",
    )(query, key, value, lse, grad_out, *turns, *marks)


def activate(gate, up, grad_act):
    sigmoid_gate = jax.nn.sigmoid(gate)
    swish = gate * sigmoid_gate
    grad_gate = grad_act * up * sigmoid_gate * (1.0 + gate * (1.0 - sigmoid_gate))
    return (swish * up).astype(BF16), grad_gate.astype(BF16), (grad_act * swish).astype(BF16)


def per_device(
    dp_size, hidden, cotangent, sequence_index, block_index, attention_gain, query_down, query_gain, query_up,
    latent_down, latent_gain, latent_up, attention_out, feedforward_gain, gate_weight, up_weight, down_weight,
):
    dp_place, row, col = lax.axis_index("dp"), lax.axis_index("row"), lax.axis_index("col")
    first_x = row == 0
    token_rows = hidden.shape[0]
    own_rows = token_rows // 2
    group_rows = sequence_index.shape[0]
    half_width = hidden.shape[1]
    heads = query_up.shape[1] // (NOPE + RD) // 2
    units = gate_weight.shape[1] // 2
    tile = group_rows // 4
    shard_order = [(a, b) for b in (0, 2) for a in (0, 1)] + [(a, b) for b in (1, 3) for a in (0, 1)]
    places = [((col ^ b) * 2 + (row ^ a)) for a, b in shard_order]

    def half_of(values, axis, which):
        length = values.shape[axis] // 2
        return lax.dynamic_slice_in_dim(values, which * length, length, axis)

    middle_plane = (dp_place == 1) | (dp_place == 2)

    def add(a, b):
        return (a.astype(F32) + b.astype(F32)).astype(BF16)

    def inward(part):
        return part, lax.ppermute(part, "dp", ((0, 1), (3, 2)))

    def across(part, arrived):
        near = add(part, arrived)
        return near, lax.ppermute(near, "dp", ((1, 2), (2, 1)))

    def outward(near, far):
        total = add(near, far)
        return total, lax.ppermute(total, "dp", ((1, 0), (2, 3)))

    def settled(total, back):
        return jnp.where(middle_plane, total, back)

    pairs = [(i, i ^ 1) for i in range(dp_size)]
    odd = dp_place % 2
    barrier = lax.optimization_barrier

    gain_in = attention_gain.astype(F32)
    hidden_wide = hidden.astype(F32)
    squares = jnp.sum(hidden_wide * hidden_wide, axis=1)[None, :]
    inverse_half = lax.rsqrt((squares + px(squares))[0] / (2 * half_width) + EPSILON)
    inverse_in = half_of(inverse_half, 0, row)
    scaled_in = hidden_wide * inverse_half[:, None]
    normed_half = (scaled_in * gain_in[None, :]).astype(BF16)

    by_factors = dp_size == 4
    every = ("dp", "row", "col")

    latent_tile = jnp.concatenate([query_down.T, latent_down.T], 0)
    tile_width = latent_tile.shape[0]
    near_tiles = jnp.concatenate([latent_tile, py(latent_tile)], 0)

    tiles = [gate_weight.T, up_weight.T, down_weight]
    count = units // dp_size
    wanted = [rows_at(t, (1 - row) * units + dp_place * count, count) for t in tiles]
    fetched = px(jnp.concatenate(wanted, 0))
    near_tiles, fetched = together(near_tiles, fetched)
    latent_weights = jnp.concatenate([near_tiles, pc(near_tiles)], 0)
    query_columns = query_up.shape[1] // 2
    w_keyval = half_of(latent_up, 1, row)

    second = jnp.sum((sequence_index == sequence_index[0]).astype(jnp.int32))
    inverse_rate = -2.0 * math.log(10000.0) / RD

    def in_order(values):
        return jnp.concatenate([rows_at(values, place * own_rows, own_rows) for place in places], 0)

    seq_all, block_all = in_order(sequence_index), in_order(block_index)
    index_all = in_order(jnp.arange(group_rows, dtype=jnp.int32))
    position = (index_all - jnp.where(seq_all == sequence_index[0], 0, second)).astype(F32)
    lane = jnp.arange(SLOT, dtype=jnp.int32)
    turning = (lane >= NOPE) & (lane < NOPE + RD)
    rate = jnp.exp(((lane - NOPE) % (RD // 2)).astype(F32) * inverse_rate)
    angle = jnp.where(turning, rate, 0.0)[None, :] * position[:, None]
    cosine, sine = jnp.cos(angle), jnp.sin(angle)
    low_sine = jnp.where(lane < NOPE + RD // 2, -sine, 0.0)
    high_sine = jnp.where(lane >= NOPE + RD // 2, sine, 0.0)
    turns = (cosine, low_sine, high_sine)
    marks = (seq_all[:, None], block_all[:, None], seq_all[None, :], block_all[None, :])
    own_cosine = cosine[:own_rows, NOPE : NOPE + RD // 2]
    own_sine = sine[:own_rows, NOPE : NOPE + RD // 2]

    latent_part = dot(normed_half, latent_weights, (1, 1))
    latent_other, query_other = together(half_of(latent_part, 0, 1 - row), half_of(query_up, 1, 1 - row))
    latent_other, query_other = px(latent_other), px(query_other)
    normed_y = py(normed_half)
    latent_raw = half_of(latent_part, 0, row) + latent_other
    others = lax.all_gather(fetched, "dp", axis=0, tiled=True)

    def in_place(values):
        blocks = [values[:, i * tile_width : (i + 1) * tile_width] for i in range(4)]
        core, high = (col % 2) == 1, (col // 2) == 1
        b0, b2, b1, b3 = blocks
        c0, c1 = jnp.where(core, b1, b0), jnp.where(core, b0, b1)
        c2, c3 = jnp.where(core, b3, b2), jnp.where(core, b2, b3)
        return (
            jnp.where(high, c2, c0), jnp.where(high, c3, c1), jnp.where(high, c0, c2), jnp.where(high, c1, c3),
        )

    blocks = in_place(latent_raw)
    query_tile = query_down.shape[1]
    query_latent = jnp.concatenate([b[:, :query_tile] for b in blocks], 1)
    kv_latent = jnp.concatenate([b[:, query_tile:] for b in blocks], 1)

    def latent_norms(query_values, key_values, query_scaling, key_scaling):
        return (
            rms_norm(query_values, query_scaling),
            rms_norm(key_values[:, :KVR], key_scaling),
            rotate(key_values[:, KVR:], own_cosine, own_sine),
        )

    own_latents, latent_back = jax.vjp(
        latent_norms, query_latent, kv_latent, query_gain.astype(F32), latent_gain.astype(F32)
    )
    side = ((0, 0), (NOPE, SLOT - NOPE - RD))
    latents_near = gather_near(jnp.concatenate([*own_latents[:2], jnp.pad(own_latents[2], side)], 1).astype(BF16))
    *latents_near, query_other = together(*latents_near, query_other)
    w_query = pair(first_x, half_of(query_up, 1, row), query_other, 0)
    w_query = jnp.pad(w_query.reshape(QR, heads, NOPE + RD), ((0, 0), (0, 0), (0, SLOT - NOPE - RD)))
    w_query = w_query.reshape(QR, heads * SLOT)
    latents = gather_core(gather_far(*latents_near))
    latents, w_query, out_late, hidden_late, cotangent_late, gain_late = together(
        latents, w_query, half_of(attention_out, 0, 1 - row), half_of(hidden, 0, 1 - row),
        half_of(cotangent, 0, 1 - row), feedforward_gain,
    )
    gain_mid = pair(first_x, feedforward_gain, px(gain_late), 0).astype(F32)
    out_other, hidden_other, cotangent_other = px(out_late), px(hidden_late), px(cotangent_late)
    compressed, latent = latents[:, :QR], latents[:, QR : QR + KVR]
    query, key, value, attended, lse = attend(
        latents, turns, w_query, w_keyval, marks, heads, tile
    )

    attended, out_other, hidden_other, cotangent_other, normed_y = together(
        attended, out_other, hidden_other, cotangent_other, normed_y
    )
    incoming = pair(first_x, half_of(cotangent, 0, row), cotangent_other, 1).astype(F32)
    grad_down_own = (RESIDUAL_SCALE * incoming).astype(BF16)
    if by_factors:
        grads_all = lax.all_gather(grad_down_own, every, axis=0, tiled=True)
    normed_rows = jnp.concatenate([normed_half, normed_y], 0)
    w_out = pair(first_x, half_of(attention_out, 0, row), out_other, 1)
    stream = pair(first_x, half_of(hidden, 0, row), hidden_other, 1).astype(F32)
    branch = scatter_core(dot(attended, w_out, (1, 0), BF16))
    middle = stream + RESIDUAL_SCALE * scatter_near(*scatter_far(branch))
    inverse_mid = lax.rsqrt(jnp.mean(middle * middle, axis=1, keepdims=True) + EPSILON)
    scaled_mid = middle * inverse_mid
    normed_mid_own = (scaled_mid * gain_mid[None, :]).astype(BF16)

    def assembled(weights, start, which):
        own = rows_at(tiles[which], row * units, units)
        weights = lax.dynamic_update_slice(weights, own, (start, row * half_width))
        for k in range(dp_size):
            other = others[(3 * k + which) * count : (3 * k + which + 1) * count]
            weights = lax.dynamic_update_slice(weights, other, (start + k * count, (1 - row) * half_width))
        return weights

    if by_factors:
        rows_all = lax.all_gather(normed_mid_own, every, axis=0, tiled=True)
    normed_near = gather_near(normed_mid_own)
    *normed_near, others, normed_rows, grad_down_own = together(*normed_near, others, normed_rows, grad_down_own)
    normed_far = gather_far(*normed_near)
    grad_down_near = gather_near(grad_down_own)
    gate_up = jnp.zeros((2 * units, 2 * half_width), BF16)
    gate_up = assembled(assembled(gate_up, 0, 0), units, 1)
    down = assembled(jnp.zeros((units, 2 * half_width), BF16), 0, 2)
    normed_mid = gather_core(normed_far)
    normed_mid, *grad_down_near = together(normed_mid, *grad_down_near)
    grad_down_far = gather_far(*grad_down_near)
    normed_rows = jnp.concatenate([normed_rows, pc(normed_rows)], 0)
    both, *grad_down_far = together(dot(gate_up, normed_mid, (1, 1)), *grad_down_far)
    grad_down = gather_core(grad_down_far)
    grad_act = dot(down, grad_down, (1, 1))
    activation, grad_gate, grad_up = activate(both[:units], both[units:], grad_act)
    activation, grad_both = together(activation, jnp.concatenate([grad_gate, grad_up], 0))

    mid_total = scatter_core(dot(grad_both, gate_up, (0, 0), BF16))
    mid_total, activation = together(mid_total, activation)
    mid_steps = scatter_far(mid_total)
    upstream_mid = scatter_near(*mid_steps)
    weighted = upstream_mid * gain_mid[None, :]
    mean_inner = jnp.mean(weighted * scaled_mid, axis=1, keepdims=True)
    gain_mid_part = jnp.sum(upstream_mid * scaled_mid, axis=0)
    grad_middle = incoming + inverse_mid * (weighted - scaled_mid * mean_inner)
    branch_near = gather_near((RESIDUAL_SCALE * grad_middle).astype(BF16))
    *branch_near, activation_late = together(*branch_near, activation)
    branch_far = gather_far(*branch_near)
    output_part = dot(activation_late, down, (0, 0), BF16)
    *branch_far, output_part = together(*branch_far, output_part)
    grad_branch = gather_core(branch_far)

    grad_attended = dot(grad_branch, w_out, (1, 1), BF16)
    out_part = dot(attended, grad_branch, (0, 0), BF16)
    grad_attended, out_part = together(grad_attended, out_part)
    out_other = px(half_of(out_part, 1, 1 - row))
    query_grad, keyval_grad, rope_grad = attend_back(
        query, key, value, lse, grad_attended, turns, marks, heads, tile
    )
    query_grad, keyval_grad, rope_grad, out_other = together(query_grad, keyval_grad, rope_grad, out_other)
    out_part = pair(first_x, half_of(out_part, 1, row), out_other, 0)
    latent_grad_part = jnp.concatenate(
        [
            dot(query_grad, w_query, (1, 1), BF16),
            dot(keyval_grad, w_keyval, (1, 1), BF16),
            rope_grad,
        ],
        1,
    )
    latent_steps = scatter_far(scatter_core(latent_grad_part))
    if by_factors:
        *latent_steps, grads_all = together(*latent_steps, grads_all)
        grad_act_all = dot(down, grads_all, (1, 1))
    latent_steps = list(latent_steps)
    latent_grad = scatter_near(*latent_steps)
    if by_factors:
        latent_grad, grad_act_all, output_part = together(latent_grad, grad_act_all, output_part)
    query_latent_grad, kv_latent_grad, query_gain_part, latent_gain_part = latent_back(
        (latent_grad[:, :QR], latent_grad[:, QR : QR + KVR], latent_grad[:, QR + KVR + NOPE : QR + KVR + NOPE + RD])
    )
    kv_tile = latent_down.shape[1]
    query_low, kv_low = query_latent_grad.astype(BF16), kv_latent_grad.astype(BF16)
    inner_in = (
        jnp.sum(query_low.astype(F32) * query_latent, axis=1) + jnp.sum(kv_low.astype(F32) * kv_latent, axis=1)
    ) / D
    in_blocks = jnp.concatenate(
        [
            part
            for i in (0, 2, 1, 3)
            for part in (
                query_low[:, i * query_tile : (i + 1) * query_tile],
                kv_low[:, i * kv_tile : (i + 1) * kv_tile],
            )
        ],
        1,
    )
    g0, g1, g2, g3 = in_place(in_blocks)
    latent_low = jnp.concatenate([g0, g2, g1, g3], 1)
    low_other, inner_other = px(latent_low), px(inner_in[None, :])[0]
    if by_factors:
        out_1 = inward(out_part)
        output_core = scatter_core(output_part)
        gate_all = dot(gate_up[:units], rows_all, (1, 1))
        low_other, gate_all, out_1, output_core = barrier((low_other, gate_all, out_1, output_core))
    latent_low = pair(first_x, latent_low, low_other, 0)
    inner_half = pair(first_x, inner_in, inner_other, 0)
    grad_normed = dot(latent_low, latent_weights, (1, 0))
    grad_middle_half = pair(
        first_x,
        half_of(grad_middle, 1, row),
        px(half_of(grad_middle, 1, 1 - row).astype(BF16)).astype(F32),
        0,
    )
    grad_in = inverse_half[:, None] * (grad_normed * gain_in[None, :] - scaled_in * inner_half[:, None])
    input_gradient = (grad_middle_half + grad_in).astype(BF16)
    gain_in_part = jnp.sum(grad_normed * scaled_in, axis=0)

    up_part = dot(compressed, query_grad, (0, 0), BF16).reshape(QR, heads, SLOT)[:, :, : NOPE + RD]
    up_part = up_part.reshape(QR, query_columns)
    up_part = pair(first_x, half_of(up_part, 0, row), px(half_of(up_part, 0, 1 - row)), 1)
    latent_up_part = dot(latent, keyval_grad, (0, 0), BF16)
    latent_up_part = pair(first_x, latent_up_part, px(latent_up_part), 1)
    low_blocks = [latent_low[:, i * tile_width : (i + 1) * tile_width] for i in range(4)]
    low_rows = jnp.concatenate([low_blocks[0], py(low_blocks[1]), pc(low_blocks[2]), pyc(low_blocks[3])], 0)
    latent_down_part = dot(low_rows, normed_rows, (0, 0), BF16)

    gains = jnp.concatenate([gain_in_part, gain_mid_part, query_gain_part, latent_gain_part]).reshape(-1, SLOT)
    gains = gains + pc(gains)
    gains = gains + py(gains)
    own_gains = half_width // SLOT
    gains = jnp.concatenate([gains[:own_gains], gains[own_gains:] + px(gains[own_gains:])], 0).reshape(-1)
    gain_count = gains.shape[0]
    gains = jnp.pad(gains, (0, -gain_count % half_width)).reshape(-1, half_width).astype(BF16)
    latent_down_part = jnp.concatenate([latent_down_part, gains], 0)
    if by_factors:
        input_gradient, up_part = barrier((input_gradient, up_part))
        out_2, up_1, output_far = across(*out_1), inward(up_part), scatter_far(output_core)
        up_all = dot(gate_up[units:], rows_all, (1, 1))
        gate_all, up_all, out_2, up_1, latent_up_part, output_far = barrier(
            (gate_all, up_all, out_2, up_1, latent_up_part, output_far)
        )
        out_3, up_2, latent_1 = outward(*out_2), across(*up_1), inward(latent_up_part)
        output_own = (middle + RESIDUAL_SCALE * scatter_near(*output_far)).astype(BF16)
        act_all, grad_gate_all, grad_up_all = activate(gate_all, up_all, grad_act_all)
        act_all, grad_gate_all, grad_up_all, up_2, latent_1, latent_down_part, output_own = barrier(
            (act_all, grad_gate_all, grad_up_all, up_2, latent_1, latent_down_part, output_own)
        )
        output = pair(first_x, half_of(output_own, 1, row), px(half_of(output_own, 1, 1 - row)), 0)
        up_3, latent_2, down_1 = outward(*up_2), across(*latent_1), inward(latent_down_part)
        own_units = units // 2

        def to_send(total):
            return rows_at(half_of(total, 1, 1 - row), odd * own_units, own_units)

        def pz(values):
            return lax.ppermute(values, "dp", pairs)

        up_total = dot(grad_up_all, rows_all, (1, 0), BF16)
        up_total, grad_gate_all, latent_2, down_1 = barrier((up_total, grad_gate_all, latent_2, down_1))
        latent_3, down_2 = outward(*latent_2), across(*down_1)
        up_other = px(to_send(up_total))
        gate_total = dot(grad_gate_all, rows_all, (1, 0), BF16)
        gate_total, act_all, down_2, up_other = barrier((gate_total, act_all, down_2, up_other))
        down_3 = outward(*down_2)
        up_far, gate_other = pz(up_other), px(to_send(gate_total))
        down_ff = dot(act_all, grads_all, (1, 0), BF16)
        down_ff, up_far, gate_other = barrier((down_ff, up_far, gate_other))
        gate_far, down_other = pz(gate_other), px(to_send(down_ff))
        unit_grads = [up_total, gate_total, down_ff]
        up_other, gate_other, down_other = (
            pair(odd == 0, other, far, 0)
            for other, far in ((up_other, up_far), (gate_other, gate_far), (down_other, pz(down_other)))
        )
        unit_others = [up_other, gate_other, down_other]
        out_grad, query_up_grad = settled(*out_3), settled(*up_3)
        latent_up_grad, down_total = settled(*latent_3), settled(*down_3)
    else:
        unit_grads = [
            lax.psum(dot(a, b, (1, 0), BF16), "dp")
            for a, b in (
                (grad_both[units:], normed_mid), (grad_both[:units], normed_mid), (activation, grad_down),
            )
        ]
        unit_others = [px(half_of(total, 1, 1 - row)) for total in unit_grads]
        output_own = (middle + RESIDUAL_SCALE * scatter_plane(output_part)).astype(BF16)
        output = pair(first_x, half_of(output_own, 1, row), px(half_of(output_own, 1, 1 - row)), 0)
        out_grad, query_up_grad, latent_up_grad, down_total = (
            lax.psum(part, "dp") for part in (out_part, up_part, latent_up_part, latent_down_part)
        )
    up_grad_t, gate_grad_t, down_grad = (
        pair(first_x, half_of(total, 1, row), other, 0).astype(F32) for total, other in zip(unit_grads, unit_others)
    )
    down_total = down_total.astype(F32)
    gain_totals = down_total[tile_width:].reshape(-1)
    gain_in_total, gain_totals = gain_totals[:half_width], gain_totals[half_width:gain_count]
    width = 2 * half_width
    return (
        output,
        input_gradient,
        gain_in_total,
        down_total[:query_tile].T,
        gain_totals[width : width + QR],
        query_up_grad.astype(F32),
        down_total[query_tile:tile_width].T,
        gain_totals[width + QR :],
        latent_up_grad.astype(F32),
        out_grad.astype(F32),
        lax.dynamic_slice_in_dim(gain_totals, row * half_width, half_width, 0),
        gate_grad_t.T,
        up_grad_t.T,
        down_grad,
    )


def solution(mesh):
    dp_size = mesh.shape["dp"]

    def program(*arguments):
        return per_device(dp_size, *arguments)

    return jax.shard_map(
        program,
        mesh=mesh,
        in_specs=(
            P(("dp", "col"), "row"),
            P(("dp", "col"), "row"),
            P("dp"),
            P("dp"),
            P("row"),
            P("row", "col"),
            P(),
            P("row", "col"),
            P("row", "col"),
            P(),
            P(None, "col"),
            P("col", "row"),
            P("row"),
            P("row", "col"),
            P("row", "col"),
            P("col", "row"),
        ),
        out_specs=(
            P(("dp", "col"), "row"),
            P(("dp", "col"), "row"),
            P("row"),
            P("row", "col"),
            P(),
            P("row", "col"),
            P("row", "col"),
            P(),
            P(None, "col"),
            P("col", "row"),
            P("row"),
            P("row", "col"),
            P("row", "col"),
            P("col", "row"),
        ),
        check_vma=False,
    )
```

```python
import math

import jax
import jax.numpy as jnp
from jax import lax
from jax.experimental import pallas as pl
from jax.experimental.pallas import tpu as pltpu
from jax.sharding import PartitionSpec as P

D = 2560
QR = 768
KVR = 256
NOPE = 64
RD = 32
VD = 64
SLOT = 128

EPSILON = 1e-05
RESIDUAL_SCALE = 1.4 / math.sqrt(62.0)
SCORE_SCALE = (NOPE + RD) ** (-0.5)
MASKED = -1000000000.0
F32 = jnp.float32
BF16 = jnp.bfloat16

OVER_X = ((0, 1), (1, 0))
OVER_CORE = ((0, 1), (1, 0), (2, 3), (3, 2))
OVER_Y = ((0, 2), (1, 3), (2, 0), (3, 1))
OVER_YCORE = ((0, 3), (1, 2), (2, 1), (3, 0))


def px(values):
    return lax.ppermute(values, "row", OVER_X)


def pc(values):
    return lax.ppermute(values, "col", OVER_CORE)


def py(values):
    return lax.ppermute(values, "col", OVER_Y)


def pyc(values):
    return lax.ppermute(values, "col", OVER_YCORE)


def dot(a, b, contract, out=F32):
    return lax.dot_general(a, b, ((contract[:1], contract[1:]), ((), ())), preferred_element_type=out)


def rows_at(values, start, length):
    return lax.dynamic_slice_in_dim(values, start, length, 0)


def pair(first_is_own, own, other, axis):
    return jnp.where(
        first_is_own,
        jnp.concatenate([own, other], axis),
        jnp.concatenate([other, own], axis),
    )


def together(*values):
    return lax.optimization_barrier(values)


def gather_near(own):
    return own, px(own), py(own)


def gather_far(own, from_x, from_y):
    half = own.shape[0] // 2
    return [own, from_x, from_y, py(from_x[:half]), px(from_y[half:])]


def gather_core(pieces):
    same_core = jnp.concatenate(pieces, 0)
    return jnp.concatenate([same_core, pc(same_core)], 0)


def gather_plane(own):
    return gather_core(gather_far(*gather_near(own)))


def scatter_core(partial):
    half = partial.shape[0] // 2
    return (partial[:half].astype(F32) + pc(partial[half:]).astype(F32)).astype(BF16)


def scatter_far(total):
    rows = total.shape[0] // 4
    half = rows // 2
    own, to_x, to_y, far = (total[i * rows : (i + 1) * rows] for i in range(4))
    return own, to_x, to_y, px(far[:half]), py(far[half:])


def scatter_near(own, to_x, to_y, for_y, for_x):
    half = for_y.shape[0]
    y_top = (to_y[:half].astype(F32) + for_y.astype(F32)).astype(BF16)
    x_low = (to_x[half:].astype(F32) + for_x.astype(F32)).astype(BF16)
    from_x = px(jnp.concatenate([to_x[:half], x_low], 0))
    from_y = py(jnp.concatenate([y_top, to_y[half:]], 0))
    return own.astype(F32) + from_x.astype(F32) + from_y.astype(F32)


def scatter_plane(partial):
    return scatter_near(*scatter_far(scatter_core(partial)))


def rms_norm(values, scaling):
    return values * lax.rsqrt(jnp.mean(values * values, axis=-1, keepdims=True) + EPSILON) * scaling


def rotate(values, cosine, sine_part):
    half_width = values.shape[-1] // 2
    first_half = values[..., :half_width]
    second_half = values[..., half_width:]
    return jnp.concatenate(
        [
            first_half * cosine - second_half * sine_part,
            second_half * cosine + first_half * sine_part,
        ],
        axis=-1,
    )


def turned(values, cosine, low_sine, high_sine):
    return (
        values * cosine
        + pltpu.roll(values, SLOT - RD // 2, 1) * low_sine
        + pltpu.roll(values, RD // 2, 1) * high_sine
    )


def allowed_bias(q_seq, q_block, k_seq, k_block):
    allowed = (q_seq == k_seq) & (k_block <= q_block)
    return jnp.where(allowed, 0.0, MASKED)


def attend_kernel(
    heads, comp, lat, rope, cosine, low_sine, high_sine, w_query, w_keyval, q_seq, q_block, k_seq, k_block,
    query_out, key_out, value_out, attended_out, lse_out,
):
    @pl.when(pl.program_id(0) == 0)
    def _():
        keyval = jnp.dot(lat[...], w_keyval[...], preferred_element_type=F32)
        lanes = lax.broadcasted_iota(jnp.int32, (lat.shape[0], SLOT), 1)
        for h in range(heads):
            part = keyval[:, h * SLOT : (h + 1) * SLOT]
            key_out[:, h * SLOT : (h + 1) * SLOT] = jnp.where(
                lanes < NOPE, part, rope[...].astype(F32)
            ).astype(BF16)
            value_out[:, h * VD : (h + 1) * VD] = part[:, NOPE:].astype(BF16)

    bias = allowed_bias(q_seq[...], q_block[...], k_seq[...], k_block[...])
    raw = jnp.dot(comp[...], w_query[...], preferred_element_type=F32)
    for h in range(heads):
        slot = slice(h * SLOT, (h + 1) * SLOT)
        query = turned(raw[:, slot], cosine[...], low_sine[...], high_sine[...]).astype(BF16)
        query_out[:, slot] = query
        scores = dot(query, key_out[:, slot], (1, 1)) * SCORE_SCALE + bias
        highest = jnp.max(scores, axis=1, keepdims=True)
        powers = jnp.exp(scores - highest)
        total = jnp.sum(powers, axis=1, keepdims=True)
        probs = (powers * (1.0 / total)).astype(BF16)
        result = jnp.dot(probs, value_out[:, h * VD : (h + 1) * VD], preferred_element_type=F32)
        attended_out[:, h * VD : (h + 1) * VD] = result.astype(BF16)
        lse_out[:, h : h + 1] = highest + jnp.log(total)


def attend_back_kernel(
    heads, query, key, value, lse, grad_out, cosine, low_sine, high_sine, q_seq, q_block, k_seq, k_block,
    query_grad, keyval_grad, rope_grad, key_total, value_total,
):
    step = pl.program_id(0)

    @pl.when(step == 0)
    def _():
        key_total[...] = jnp.zeros_like(key_total)
        value_total[...] = jnp.zeros_like(value_total)

    bias = allowed_bias(q_seq[...], q_block[...], k_seq[...], k_block[...])
    for h in range(heads):
        slot = slice(h * SLOT, (h + 1) * SLOT)
        narrow = slice(h * VD, (h + 1) * VD)
        scores = dot(query[:, slot], key[:, slot], (1, 1)) * SCORE_SCALE + bias
        probs = jnp.exp(scores - lse[:, h : h + 1])
        grad_probs = dot(grad_out[:, narrow], value[:, narrow], (1, 1))
        inner = jnp.sum(probs * grad_probs, axis=1, keepdims=True)
        grad_dots = (probs * (grad_probs - inner) * SCORE_SCALE).astype(BF16)
        back = jnp.dot(grad_dots, key[:, slot], preferred_element_type=F32)
        query_grad[:, slot] = turned(back, cosine[...], -low_sine[...], -high_sine[...]).astype(BF16)
        key_total[:, slot] += dot(grad_dots, query[:, slot], (0, 0))
        value_total[:, narrow] += dot(probs.astype(BF16), grad_out[:, narrow], (0, 0))

    @pl.when(step == pl.num_programs(0) - 1)
    def _():
        rope_total = jnp.zeros((key.shape[0], SLOT), F32)
        for h in range(heads):
            part = key_total[:, h * SLOT : (h + 1) * SLOT]
            rope_total = rope_total + part
            keyval_grad[:, h * SLOT : h * SLOT + NOPE] = part[:, :NOPE].astype(BF16)
            keyval_grad[:, h * SLOT + NOPE : (h + 1) * SLOT] = value_total[:, h * VD : (h + 1) * VD].astype(BF16)
        lanes = lax.broadcasted_iota(jnp.int32, rope_total.shape, 1)
        rope_grad[...] = jnp.where(lanes >= NOPE, rope_total, 0.0).astype(BF16)


def row_tile(rows, width):
    return pl.BlockSpec((rows, width), lambda i: (i, 0))


def whole(shape):
    return pl.BlockSpec(shape, lambda i: (0, 0))


def attend(latents, turns, w_query, w_keyval, marks, heads, tile):
    rows = latents.shape[0]
    column = row_tile(tile, 1)
    line = whole((1, rows))
    return pl.pallas_call(
        lambda *refs: attend_kernel(heads, *refs),
        grid=(rows // tile,),
        in_specs=[
            row_tile(tile, QR), pl.BlockSpec((rows, KVR), lambda i: (0, QR // KVR)),
            pl.BlockSpec((rows, SLOT), lambda i: (0, (QR + KVR) // SLOT)),
            row_tile(tile, SLOT), row_tile(tile, SLOT), row_tile(tile, SLOT),
            whole(w_query.shape), whole(w_keyval.shape), column, column, line, line,
        ],
        out_specs=[
            row_tile(tile, heads * SLOT), whole((rows, heads * SLOT)), whole((rows, heads * VD)),
            row_tile(tile, heads * VD), row_tile(tile, 8),
        ],
        out_shape=[
            jax.ShapeDtypeStruct((rows, heads * SLOT), BF16),
            jax.ShapeDtypeStruct((rows, heads * SLOT), BF16),
            jax.ShapeDtypeStruct((rows, heads * VD), BF16),
            jax.ShapeDtypeStruct((rows, heads * VD), BF16),
            jax.ShapeDtypeStruct((rows, 8), F32),
        ],
        compiler_params=pltpu.CompilerParams(vmem_limit_bytes=48 << 20),
        cost_estimate=pl.CostEstimate(
            flops=2 * rows * heads * (rows * 2 * SLOT + QR * SLOT), bytes_accessed=8 << 20,
            transcendentals=heads * rows * rows,
        ),
        name="attend",
    )(latents, latents, latents, *turns, w_query, w_keyval, *marks)


def attend_back(query, key, value, lse, grad_out, turns, marks, heads, tile):
    rows = query.shape[0]
    column = row_tile(tile, 1)
    line = whole((1, rows))
    return pl.pallas_call(
        lambda *refs: attend_back_kernel(heads, *refs),
        grid=(rows // tile,),
        in_specs=[
            row_tile(tile, heads * SLOT), whole((rows, heads * SLOT)), whole((rows, heads * VD)),
            row_tile(tile, 8), row_tile(tile, heads * VD),
            row_tile(tile, SLOT), row_tile(tile, SLOT), row_tile(tile, SLOT), column, column, line, line,
        ],
        out_specs=[
            row_tile(tile, heads * SLOT), whole((rows, heads * SLOT)), whole((rows, SLOT)),
        ],
        out_shape=[
            jax.ShapeDtypeStruct((rows, heads * SLOT), BF16),
            jax.ShapeDtypeStruct((rows, heads * SLOT), BF16),
            jax.ShapeDtypeStruct((rows, SLOT), BF16),
        ],
        scratch_shapes=[pltpu.VMEM((rows, heads * SLOT), F32), pltpu.VMEM((rows, heads * VD), F32)],
        compiler_params=pltpu.CompilerParams(vmem_limit_bytes=48 << 20),
        cost_estimate=pl.CostEstimate(
            flops=2 * rows * heads * rows * 5 * SLOT, bytes_accessed=8 << 20, transcendentals=heads * rows * rows,
        ),
        name="attend_back",
    )(query, key, value, lse, grad_out, *turns, *marks)


def activate(gate, up, grad_act):
    sigmoid_gate = jax.nn.sigmoid(gate)
    swish = gate * sigmoid_gate
    grad_gate = grad_act * up * sigmoid_gate * (1.0 + gate * (1.0 - sigmoid_gate))
    return (swish * up).astype(BF16), grad_gate.astype(BF16), (grad_act * swish).astype(BF16)


def per_device(
    dp_size, hidden, cotangent, sequence_index, block_index, attention_gain, query_down, query_gain, query_up,
    latent_down, latent_gain, latent_up, attention_out, feedforward_gain, gate_weight, up_weight, down_weight,
):
    dp_place, row, col = lax.axis_index("dp"), lax.axis_index("row"), lax.axis_index("col")
    first_x = row == 0
    token_rows = hidden.shape[0]
    own_rows = token_rows // 2
    group_rows = sequence_index.shape[0]
    half_width = hidden.shape[1]
    heads = query_up.shape[1] // (NOPE + RD) // 2
    units = gate_weight.shape[1] // 2
    tile = group_rows // 4
    shard_order = [(a, b) for b in (0, 2) for a in (0, 1)] + [(a, b) for b in (1, 3) for a in (0, 1)]
    places = [((col ^ b) * 2 + (row ^ a)) for a, b in shard_order]

    def half_of(values, axis, which):
        length = values.shape[axis] // 2
        return lax.dynamic_slice_in_dim(values, which * length, length, axis)

    middle_plane = (dp_place == 1) | (dp_place == 2)

    def add(a, b):
        return (a.astype(F32) + b.astype(F32)).astype(BF16)

    def inward(part):
        return part, lax.ppermute(part, "dp", ((0, 1), (3, 2)))

    def across(part, arrived):
        near = add(part, arrived)
        return near, lax.ppermute(near, "dp", ((1, 2), (2, 1)))

    def outward(near, far):
        total = add(near, far)
        return total, lax.ppermute(total, "dp", ((1, 0), (2, 3)))

    def settled(total, back):
        return jnp.where(middle_plane, total, back)

    pairs = [(i, i ^ 1) for i in range(dp_size)]
    odd = dp_place % 2
    barrier = lax.optimization_barrier

    gain_in = attention_gain.astype(F32)
    hidden_wide = hidden.astype(F32)
    squares = jnp.sum(hidden_wide * hidden_wide, axis=1)[None, :]
    inverse_half = lax.rsqrt((squares + px(squares))[0] / (2 * half_width) + EPSILON)
    inverse_in = half_of(inverse_half, 0, row)
    scaled_in = hidden_wide * inverse_half[:, None]
    normed_half = (scaled_in * gain_in[None, :]).astype(BF16)

    by_factors = dp_size == 4
    every = ("dp", "row", "col")

    latent_tile = jnp.concatenate([query_down.T, latent_down.T], 0)
    tile_width = latent_tile.shape[0]
    near_tiles = jnp.concatenate([latent_tile, py(latent_tile)], 0)

    tiles = [gate_weight.T, up_weight.T, down_weight]
    count = units // dp_size
    wanted = [rows_at(t, (1 - row) * units + dp_place * count, count) for t in tiles]
    fetched = px(jnp.concatenate(wanted, 0))
    near_tiles, fetched = together(near_tiles, fetched)
    latent_weights = jnp.concatenate([near_tiles, pc(near_tiles)], 0)
    query_columns = query_up.shape[1] // 2
    w_keyval = half_of(latent_up, 1, row)

    second = jnp.sum((sequence_index == sequence_index[0]).astype(jnp.int32))
    inverse_rate = -2.0 * math.log(10000.0) / RD

    def in_order(values):
        return jnp.concatenate([rows_at(values, place * own_rows, own_rows) for place in places], 0)

    seq_all, block_all = in_order(sequence_index), in_order(block_index)
    index_all = in_order(jnp.arange(group_rows, dtype=jnp.int32))
    position = (index_all - jnp.where(seq_all == sequence_index[0], 0, second)).astype(F32)
    lane = jnp.arange(SLOT, dtype=jnp.int32)
    turning = (lane >= NOPE) & (lane < NOPE + RD)
    rate = jnp.exp(((lane - NOPE) % (RD // 2)).astype(F32) * inverse_rate)
    angle = jnp.where(turning, rate, 0.0)[None, :] * position[:, None]
    cosine, sine = jnp.cos(angle), jnp.sin(angle)
    low_sine = jnp.where(lane < NOPE + RD // 2, -sine, 0.0)
    high_sine = jnp.where(lane >= NOPE + RD // 2, sine, 0.0)
    turns = (cosine, low_sine, high_sine)
    marks = (seq_all[:, None], block_all[:, None], seq_all[None, :], block_all[None, :])
    own_cosine = cosine[:own_rows, NOPE : NOPE + RD // 2]
    own_sine = sine[:own_rows, NOPE : NOPE + RD // 2]

    latent_part = dot(normed_half, latent_weights, (1, 1))
    latent_other, query_other = together(half_of(latent_part, 0, 1 - row), half_of(query_up, 1, 1 - row))
    latent_other, query_other = px(latent_other), px(query_other)
    normed_y = py(normed_half)
    latent_raw = half_of(latent_part, 0, row) + latent_other
    others = lax.all_gather(fetched, "dp", axis=0, tiled=True)

    def in_place(values):
        blocks = [values[:, i * tile_width : (i + 1) * tile_width] for i in range(4)]
        core, high = (col % 2) == 1, (col // 2) == 1
        b0, b2, b1, b3 = blocks
        c0, c1 = jnp.where(core, b1, b0), jnp.where(core, b0, b1)
        c2, c3 = jnp.where(core, b3, b2), jnp.where(core, b2, b3)
        return (
            jnp.where(high, c2, c0), jnp.where(high, c3, c1), jnp.where(high, c0, c2), jnp.where(high, c1, c3),
        )

    blocks = in_place(latent_raw)
    query_tile = query_down.shape[1]
    query_latent = jnp.concatenate([b[:, :query_tile] for b in blocks], 1)
    kv_latent = jnp.concatenate([b[:, query_tile:] for b in blocks], 1)

    def latent_norms(query_values, key_values, query_scaling, key_scaling):
        return (
            rms_norm(query_values, query_scaling),
            rms_norm(key_values[:, :KVR], key_scaling),
            rotate(key_values[:, KVR:], own_cosine, own_sine),
        )

    own_latents, latent_back = jax.vjp(
        latent_norms, query_latent, kv_latent, query_gain.astype(F32), latent_gain.astype(F32)
    )
    side = ((0, 0), (NOPE, SLOT - NOPE - RD))
    latents_near = gather_near(jnp.concatenate([*own_latents[:2], jnp.pad(own_latents[2], side)], 1).astype(BF16))
    *latents_near, query_other = together(*latents_near, query_other)
    w_query = pair(first_x, half_of(query_up, 1, row), query_other, 0)
    w_query = jnp.pad(w_query.reshape(QR, heads, NOPE + RD), ((0, 0), (0, 0), (0, SLOT - NOPE - RD)))
    w_query = w_query.reshape(QR, heads * SLOT)
    latents = gather_core(gather_far(*latents_near))
    latents, w_query, out_late, hidden_late, cotangent_late, gain_late = together(
        latents, w_query, half_of(attention_out, 0, 1 - row), half_of(hidden, 0, 1 - row),
        half_of(cotangent, 0, 1 - row), feedforward_gain,
    )
    gain_mid = pair(first_x, feedforward_gain, px(gain_late), 0).astype(F32)
    out_other, hidden_other, cotangent_other = px(out_late), px(hidden_late), px(cotangent_late)
    compressed, latent = latents[:, :QR], latents[:, QR : QR + KVR]
    query, key, value, attended, lse = attend(
        latents, turns, w_query, w_keyval, marks, heads, tile
    )

    attended, out_other, hidden_other, cotangent_other, normed_y = together(
        attended, out_other, hidden_other, cotangent_other, normed_y
    )
    incoming = pair(first_x, half_of(cotangent, 0, row), cotangent_other, 1).astype(F32)
    grad_down_own = (RESIDUAL_SCALE * incoming).astype(BF16)
    if by_factors:
        grads_all = lax.all_gather(grad_down_own, every, axis=0, tiled=True)
    normed_rows = jnp.concatenate([normed_half, normed_y], 0)
    w_out = pair(first_x, half_of(attention_out, 0, row), out_other, 1)
    stream = pair(first_x, half_of(hidden, 0, row), hidden_other, 1).astype(F32)
    branch = scatter_core(dot(attended, w_out, (1, 0), BF16))
    middle = stream + RESIDUAL_SCALE * scatter_near(*scatter_far(branch))
    inverse_mid = lax.rsqrt(jnp.mean(middle * middle, axis=1, keepdims=True) + EPSILON)
    scaled_mid = middle * inverse_mid
    normed_mid_own = (scaled_mid * gain_mid[None, :]).astype(BF16)

    def assembled(weights, start, which):
        own = rows_at(tiles[which], row * units, units)
        weights = lax.dynamic_update_slice(weights, own, (start, row * half_width))
        for k in range(dp_size):
            other = others[(3 * k + which) * count : (3 * k + which + 1) * count]
            weights = lax.dynamic_update_slice(weights, other, (start + k * count, (1 - row) * half_width))
        return weights

    if by_factors:
        rows_all = lax.all_gather(normed_mid_own, every, axis=0, tiled=True)
    normed_near = gather_near(normed_mid_own)
    *normed_near, others, normed_rows, grad_down_own = together(*normed_near, others, normed_rows, grad_down_own)
    normed_far = gather_far(*normed_near)
    grad_down_near = gather_near(grad_down_own)
    gate_up = jnp.zeros((2 * units, 2 * half_width), BF16)
    gate_up = assembled(assembled(gate_up, 0, 0), units, 1)
    down = assembled(jnp.zeros((units, 2 * half_width), BF16), 0, 2)
    normed_mid = gather_core(normed_far)
    normed_mid, *grad_down_near = together(normed_mid, *grad_down_near)
    grad_down_far = gather_far(*grad_down_near)
    normed_rows = jnp.concatenate([normed_rows, pc(normed_rows)], 0)
    both, *grad_down_far = together(dot(gate_up, normed_mid, (1, 1)), *grad_down_far)
    grad_down = gather_core(grad_down_far)
    grad_act = dot(down, grad_down, (1, 1))
    activation, grad_gate, grad_up = activate(both[:units], both[units:], grad_act)
    activation, grad_both = together(activation, jnp.concatenate([grad_gate, grad_up], 0))

    mid_total = scatter_core(dot(grad_both, gate_up, (0, 0), BF16))
    mid_total, activation = together(mid_total, activation)
    mid_steps = scatter_far(mid_total)
    upstream_mid = scatter_near(*mid_steps)
    weighted = upstream_mid * gain_mid[None, :]
    mean_inner = jnp.mean(weighted * scaled_mid, axis=1, keepdims=True)
    gain_mid_part = jnp.sum(upstream_mid * scaled_mid, axis=0)
    grad_middle = incoming + inverse_mid * (weighted - scaled_mid * mean_inner)
    branch_near = gather_near((RESIDUAL_SCALE * grad_middle).astype(BF16))
    *branch_near, activation_late = together(*branch_near, activation)
    branch_far = gather_far(*branch_near)
    output_part = dot(activation_late, down, (0, 0), BF16)
    *branch_far, output_part = together(*branch_far, output_part)
    grad_branch = gather_core(branch_far)

    grad_attended = dot(grad_branch, w_out, (1, 1), BF16)
    out_part = dot(attended, grad_branch, (0, 0), BF16)
    grad_attended, out_part = together(grad_attended, out_part)
    out_other = px(half_of(out_part, 1, 1 - row))
    query_grad, keyval_grad, rope_grad = attend_back(
        query, key, value, lse, grad_attended, turns, marks, heads, tile
    )
    query_grad, keyval_grad, rope_grad, out_other = together(query_grad, keyval_grad, rope_grad, out_other)
    out_part = pair(first_x, half_of(out_part, 1, row), out_other, 0)
    latent_grad_part = jnp.concatenate(
        [
            dot(query_grad, w_query, (1, 1), BF16),
            dot(keyval_grad, w_keyval, (1, 1), BF16),
            rope_grad,
        ],
        1,
    )
    latent_steps = scatter_far(scatter_core(latent_grad_part))
    if by_factors:
        *latent_steps, grads_all = together(*latent_steps, grads_all)
        grad_act_all = dot(down, grads_all, (1, 1), BF16)
    latent_steps = list(latent_steps)
    latent_grad = scatter_near(*latent_steps)
    if by_factors:
        latent_grad, grad_act_all, output_part = together(latent_grad, grad_act_all, output_part)
    query_latent_grad, kv_latent_grad, query_gain_part, latent_gain_part = latent_back(
        (latent_grad[:, :QR], latent_grad[:, QR : QR + KVR], latent_grad[:, QR + KVR + NOPE : QR + KVR + NOPE + RD])
    )
    kv_tile = latent_down.shape[1]
    query_low, kv_low = query_latent_grad.astype(BF16), kv_latent_grad.astype(BF16)
    inner_in = (
        jnp.sum(query_low.astype(F32) * query_latent, axis=1) + jnp.sum(kv_low.astype(F32) * kv_latent, axis=1)
    ) / D
    in_blocks = jnp.concatenate(
        [
            part
            for i in (0, 2, 1, 3)
            for part in (
                query_low[:, i * query_tile : (i + 1) * query_tile],
                kv_low[:, i * kv_tile : (i + 1) * kv_tile],
            )
        ],
        1,
    )
    g0, g1, g2, g3 = in_place(in_blocks)
    latent_low = jnp.concatenate([g0, g2, g1, g3], 1)
    low_other, inner_other = px(latent_low), px(inner_in[None, :])[0]
    if by_factors:
        out_1 = inward(out_part)
        output_core = scatter_core(output_part)
        gate_all = dot(gate_up[:units], rows_all, (1, 1), BF16)
        low_other, gate_all, out_1, output_core = barrier((low_other, gate_all, out_1, output_core))
    latent_low = pair(first_x, latent_low, low_other, 0)
    inner_half = pair(first_x, inner_in, inner_other, 0)
    grad_normed = dot(latent_low, latent_weights, (1, 0))
    grad_middle_half = pair(
        first_x,
        half_of(grad_middle, 1, row),
        px(half_of(grad_middle, 1, 1 - row).astype(BF16)).astype(F32),
        0,
    )
    grad_in = inverse_half[:, None] * (grad_normed * gain_in[None, :] - scaled_in * inner_half[:, None])
    input_gradient = (grad_middle_half + grad_in).astype(BF16)
    gain_in_part = jnp.sum(grad_normed * scaled_in, axis=0)

    up_part = dot(compressed, query_grad, (0, 0), BF16).reshape(QR, heads, SLOT)[:, :, : NOPE + RD]
    up_part = up_part.reshape(QR, query_columns)
    up_part = pair(first_x, half_of(up_part, 0, row), px(half_of(up_part, 0, 1 - row)), 1)
    latent_up_part = dot(latent, keyval_grad, (0, 0), BF16)
    latent_up_part = pair(first_x, latent_up_part, px(latent_up_part), 1)
    low_blocks = [latent_low[:, i * tile_width : (i + 1) * tile_width] for i in range(4)]
    low_rows = jnp.concatenate([low_blocks[0], py(low_blocks[1]), pc(low_blocks[2]), pyc(low_blocks[3])], 0)
    latent_down_part = dot(low_rows, normed_rows, (0, 0), BF16)

    gains = jnp.concatenate([gain_in_part, gain_mid_part, query_gain_part, latent_gain_part]).reshape(-1, SLOT)
    gains = gains + pc(gains)
    gains = gains + py(gains)
    own_gains = half_width // SLOT
    gains = jnp.concatenate([gains[:own_gains], gains[own_gains:] + px(gains[own_gains:])], 0).reshape(-1)
    gain_count = gains.shape[0]
    gains = jnp.pad(gains, (0, -gain_count % half_width)).reshape(-1, half_width).astype(BF16)
    latent_down_part = jnp.concatenate([latent_down_part, gains], 0)
    if by_factors:
        input_gradient, up_part = barrier((input_gradient, up_part))
        out_2, up_1, output_far = across(*out_1), inward(up_part), scatter_far(output_core)
        up_all = dot(gate_up[units:], rows_all, (1, 1), BF16)
        gate_all, up_all, out_2, up_1, latent_up_part, output_far = barrier(
            (gate_all, up_all, out_2, up_1, latent_up_part, output_far)
        )
        out_3, up_2, latent_1 = outward(*out_2), across(*up_1), inward(latent_up_part)
        output_own = (middle + RESIDUAL_SCALE * scatter_near(*output_far)).astype(BF16)
        act_all, grad_gate_all, grad_up_all = activate(*(v.astype(F32) for v in (gate_all, up_all, grad_act_all)))
        act_all, grad_gate_all, grad_up_all, up_2, latent_1, latent_down_part, output_own = barrier(
            (act_all, grad_gate_all, grad_up_all, up_2, latent_1, latent_down_part, output_own)
        )
        output = pair(first_x, half_of(output_own, 1, row), px(half_of(output_own, 1, 1 - row)), 0)
        up_3, latent_2, down_1 = outward(*up_2), across(*latent_1), inward(latent_down_part)
        own_units = units // 2

        def to_send(total):
            return rows_at(half_of(total, 1, 1 - row), odd * own_units, own_units)

        def pz(values):
            return lax.ppermute(values, "dp", pairs)

        up_total = dot(grad_up_all, rows_all, (1, 0), BF16)
        up_total, grad_gate_all, latent_2, down_1 = barrier((up_total, grad_gate_all, latent_2, down_1))
        latent_3, down_2 = outward(*latent_2), across(*down_1)
        up_other = px(to_send(up_total))
        gate_total = dot(grad_gate_all, rows_all, (1, 0), BF16)
        gate_total, act_all, down_2, up_other = barrier((gate_total, act_all, down_2, up_other))
        down_3 = outward(*down_2)
        up_far, gate_other = pz(up_other), px(to_send(gate_total))
        down_ff = dot(act_all, grads_all, (1, 0), BF16)
        down_ff, up_far, gate_other = barrier((down_ff, up_far, gate_other))
        gate_far, down_other = pz(gate_other), px(to_send(down_ff))
        unit_grads = [up_total, gate_total, down_ff]
        up_other, gate_other, down_other = (
            pair(odd == 0, other, far, 0)
            for other, far in ((up_other, up_far), (gate_other, gate_far), (down_other, pz(down_other)))
        )
        unit_others = [up_other, gate_other, down_other]
        out_grad, query_up_grad = settled(*out_3), settled(*up_3)
        latent_up_grad, down_total = settled(*latent_3), settled(*down_3)
    else:
        unit_grads = [
            lax.psum(dot(a, b, (1, 0), BF16), "dp")
            for a, b in (
                (grad_both[units:], normed_mid), (grad_both[:units], normed_mid), (activation, grad_down),
            )
        ]
        unit_others = [px(half_of(total, 1, 1 - row)) for total in unit_grads]
        output_own = (middle + RESIDUAL_SCALE * scatter_plane(output_part)).astype(BF16)
        output = pair(first_x, half_of(output_own, 1, row), px(half_of(output_own, 1, 1 - row)), 0)
        out_grad, query_up_grad, latent_up_grad, down_total = (
            lax.psum(part, "dp") for part in (out_part, up_part, latent_up_part, latent_down_part)
        )
    up_grad_t, gate_grad_t, down_grad = (
        pair(first_x, half_of(total, 1, row), other, 0).astype(F32) for total, other in zip(unit_grads, unit_others)
    )
    down_total = down_total.astype(F32)
    gain_totals = down_total[tile_width:].reshape(-1)
    gain_in_total, gain_totals = gain_totals[:half_width], gain_totals[half_width:gain_count]
    width = 2 * half_width
    return (
        output,
        input_gradient,
        gain_in_total,
        down_total[:query_tile].T,
        gain_totals[width : width + QR],
        query_up_grad.astype(F32),
        down_total[query_tile:tile_width].T,
        gain_totals[width + QR :],
        latent_up_grad.astype(F32),
        out_grad.astype(F32),
        lax.dynamic_slice_in_dim(gain_totals, row * half_width, half_width, 0),
        gate_grad_t.T,
        up_grad_t.T,
        down_grad,
    )


def solution(mesh):
    dp_size = mesh.shape["dp"]

    def program(*arguments):
        return per_device(dp_size, *arguments)

    return jax.shard_map(
        program,
        mesh=mesh,
        in_specs=(
            P(("dp", "col"), "row"),
            P(("dp", "col"), "row"),
            P("dp"),
            P("dp"),
            P("row"),
            P("row", "col"),
            P(),
            P("row", "col"),
            P("row", "col"),
            P(),
            P(None, "col"),
            P("col", "row"),
            P("row"),
            P("row", "col"),
            P("row", "col"),
            P("col", "row"),
        ),
        out_specs=(
            P(("dp", "col"), "row"),
            P(("dp", "col"), "row"),
            P("row"),
            P("row", "col"),
            P(),
            P("row", "col"),
            P("row", "col"),
            P(),
            P(None, "col"),
            P("col", "row"),
            P("row"),
            P("row", "col"),
            P("row", "col"),
            P("col", "row"),
        ),
        check_vma=False,
    )
```
